32 devices in a mesh: grp: 2 (over y), hh: 4 (over z), per: 2 (over x), st: 2 (over core).
Axes of the slice: x: 2, y: 2, z: 4, core: 2. Of those that a mesh axis runs over, the one named last changes fastest.
Arguments:
- earnings: float32 [3072, 16], P(('hh', 'per')), may hold values from -5.4 to 5.4
- starts: int32 [3072], P(('hh', 'per')), may hold values from 0 to 12, as said below
- lengths: int32 [3072], P(('hh', 'per')), may hold values from 4 to 16
- block_count: int32 [8], P(('hh', 'per')), may hold values from 0 to 3, as said below
- trans_logits: bfloat16 [32, 256, 256], P(('grp', 'per', 'st')), parts along dimension 0, may hold values from -4 to 4
- init_logits: float32 [512], P('grp'), parts along dimension 0, may hold values from -4 to 4
- state_mean: float32 [512], P('grp'), parts along dimension 0, may hold values from -4 to 4
- log_sd: float32 [512], P('grp'), parts along dimension 0, may hold values from 0 to 1
Outputs:
- trans_grad: float32 [32, 256, 256], P(('grp', 'per'), 'hh', 'st'), parts along dimension 0
- mean_loglik: float32 [2], P('grp'), parts along dimension 0
The draws below stay inside these ranges and needn't reach their ends.
There are 2 independent parts, one for each index of `grp`. The reference program is written for one: setup_inputs(seed, part) draws one part's arguments, and reference() takes and returns one part's arrays. A program takes and returns all parts, laid end to end along the dimension named above; an argument that names none is the same for every part. Nothing has to cross between parts.
Inputs may be any that keep to these rules, and one draw needn't show every extreme that they name: starts[h] + lengths[h] <= 16. Exactly 1 device hold 3 blocks and as many hold 2; the counts sum to 8. Only the first block_count[d] blocks of device d's 3 slots hold households; the entries of the other slots are to be ignored.
All inputs are finite; a program needn't handle non-finite values.
Results may differ from the reference program's by a relative error of at most 0.00055.
Values may be sent and summed in bfloat16 or wider, within the bound.
A program may use at most 64 MiB of HBM per device.

```python
import jax
import jax.numpy as jnp
from jax import lax

S = 256
NT = 16
HB = 128
CAP = 3
ND = 8


def draw_earnings(key, part):
    row_count = CAP * HB * ND
    slot_ids = jnp.arange(row_count, dtype=jnp.int32)
    device_ids = slot_ids // (CAP * HB)
    cycle_pos = slot_ids % (CAP * HB) % ND
    level_exp = (device_ids + cycle_pos).astype(jnp.float32) / ND
    row_scale = 0.3 * 3.0 ** level_exp
    base_draw = jnp.clip(jax.random.normal(key, (row_count, NT), jnp.float32), -2.0, 2.0)
    return base_draw * row_scale[:, None]


def household_times(key):
    row_count = CAP * HB * ND
    slot_ids = jnp.arange(row_count, dtype=jnp.int32)
    span_len = jax.random.randint(jax.random.fold_in(key, 101), (row_count,), 4, NT + 1)
    span_len = jnp.where(slot_ids == 0, NT, jnp.where(slot_ids == 1, 4, span_len))
    raw_bits = jax.random.randint(jax.random.fold_in(key, 202), (row_count,), 0, 1 << 20)
    begin_at = raw_bits % (NT - span_len + 1)
    begin_at = jnp.where(slot_ids == 1, NT - 4, begin_at)
    return (begin_at.astype(jnp.int32), span_len.astype(jnp.int32))


def draw_starts(key, part):
    return household_times(key)[0]


def draw_lengths(key, part):
    return household_times(key)[1]


def draw_block_count(key, part):
    eighth = ND // 8
    rank_ids = jnp.arange(ND, dtype=jnp.int32)
    count_table = jnp.where(rank_ids < eighth, CAP, jnp.where(rank_ids < CAP * eighth, 0, jnp.where(rank_ids < CAP * eighth + eighth, 2, jnp.where(rank_ids < CAP * eighth + 2 * eighth, 0, 1))))
    shuffle = jax.random.permutation(key, ND)
    return count_table[shuffle].astype(jnp.int32)


def block_levels(rng, shape, split, smallest, largest):
    def one(axis_at, blocks):
        steps = jax.random.uniform(jax.random.fold_in(jax.random.fold_in(rng, 6), axis_at), (blocks,), jnp.float32, smallest / len(split), largest / len(split))
        return jnp.repeat(jnp.exp(steps), shape[axis_at] // blocks).reshape((-1,) + (1,) * (len(shape) - axis_at - 1))

    level = one(*split[0])
    for cut in split[1:]:
        level = level * one(*cut)
    return level


def scatter_about(stream_key, extent, deviation, most, pieces=(), kind=jnp.bfloat16):
    factor_of = block_levels(stream_key, extent, pieces, -0.22, 0.18) if pieces else 1.0
    result = jax.random.normal(stream_key, extent, jnp.float32) * deviation * factor_of
    return jnp.minimum(jnp.maximum(result, -most), most).astype(kind)


def setup_inputs(seed: int = 0, part: int = 0) -> dict:
    streams_of = jax.random.split(jax.random.key(seed), 9)
    part_splits = jax.random.split(jax.random.fold_in(streams_of[8], part), 9)
    return {
        "earnings": draw_earnings(jax.random.fold_in(streams_of[8], 71), part),
        "starts": draw_starts(jax.random.fold_in(streams_of[8], 71), part),
        "lengths": draw_lengths(jax.random.fold_in(streams_of[8], 71), part),
        "block_count": draw_block_count(jax.random.fold_in(streams_of[8], 71), part),
        "trans_logits": scatter_about(part_splits[4], (NT, S, S), 1.0, 4.0, ((0, 4),)),
        "init_logits": scatter_about(part_splits[5], (S,), 1.0, 4.0, (), jnp.float32),
        "state_mean": jnp.clip(jax.random.uniform(part_splits[6], (S,), jnp.float32, -4.0, 4.0), -4.0, 4.0),
        "log_sd": jnp.clip(jax.random.uniform(part_splits[7], (S,), jnp.float32, 0.0, 1.0), 0.0, 1.0),
    }


top_precision = lax.Precision.HIGHEST


def emission(column, state_mean, log_sd):
    z_score = (column[:, None] - state_mean[None, :]) / jnp.exp(log_sd)[None, :]
    return jnp.exp(-0.5 * z_score * z_score - log_sd[None, :])


def reference(earnings, starts, lengths, block_count, trans_logits, init_logits, state_mean, log_sd):
    raised = jnp.exp(trans_logits.astype(jnp.float32))
    probs = raised / jnp.sum(raised, axis=2, keepdims=True)
    raised_first = jnp.exp(init_logits)
    first_probs = raised_first / jnp.sum(raised_first)
    num_states = first_probs.shape[0]
    block_total = ND * CAP
    block_alive = (jnp.arange(block_total, dtype=jnp.int32) % CAP) < jnp.repeat(block_count, CAP)
    earn_blocks = earnings.reshape(block_total, HB, NT)
    start_blocks = starts.reshape(block_total, HB)
    length_blocks = lengths.reshape(block_total, HB)
    period_ids = jnp.arange(NT, dtype=jnp.int32)

    def block_terms(earn_rows, begin_at, span_len):
        def forward(prev_alpha, inputs):
            matrix, column, step_now = inputs
            moved_mass = jnp.dot(prev_alpha, matrix, precision=top_precision, preferred_element_type=jnp.float32)
            joint_mass = jnp.where((step_now <= begin_at)[:, None], first_probs[None, :], moved_mass) * emission(column, state_mean, log_sd)
            seen_now = (step_now >= begin_at) & (step_now < begin_at + span_len)
            scale_now = jnp.where(seen_now, jnp.sum(joint_mass, axis=1), 1.0)
            new_alpha = jnp.where(seen_now[:, None], joint_mass / scale_now[:, None], prev_alpha)
            return new_alpha, (new_alpha, scale_now)

        start_alpha = jnp.broadcast_to(first_probs[None, :], (HB, num_states))
        columns = earn_rows.T
        _, (alphas, scales) = lax.scan(forward, start_alpha, (probs, columns, period_ids))

        def carry_of(back_now, column, scale_now, step_now):
            seen_now = (step_now >= begin_at) & (step_now < begin_at + span_len)
            return jnp.where(seen_now[:, None], emission(column, state_mean, log_sd) * back_now / scale_now[:, None], 0.0)

        def backward(carry_now, inputs):
            matrix, alpha_prev, column_prev, scale_prev, step_now = inputs
            moving = (step_now > begin_at) & (step_now < begin_at + span_len)
            weights = jnp.where(moving[:, None], alpha_prev, 0.0)
            grad_term = jnp.dot(weights.T, carry_now, precision=top_precision, preferred_element_type=jnp.float32)
            back_now = jnp.where(moving[:, None], jnp.dot(carry_now, matrix.T, precision=top_precision, preferred_element_type=jnp.float32), 1.0)
            return carry_of(back_now, column_prev, scale_prev, step_now - 1), grad_term

        last_carry = carry_of(jnp.ones((HB, num_states), jnp.float32), columns[NT - 1], scales[NT - 1], NT - 1)
        _, grad_terms = lax.scan(backward, last_carry, (probs[1:], alphas[:-1], columns[:-1], scales[:-1], period_ids[1:]), reverse=True)
        return grad_terms, jnp.sum(jnp.log(scales)), jnp.sum(span_len).astype(jnp.float32)

    def accumulate(totals, inputs):
        earn_rows, begin_at, span_len, alive_now = inputs

        def take_block(operands):
            counts, loglik, years = totals
            grad_terms, part_loglik, part_years = block_terms(operands[0], operands[1], operands[2])
            return counts.at[1:].add(grad_terms), loglik + part_loglik, years + part_years

        def skip_block(operands):
            return totals

        return lax.cond(alive_now, take_block, skip_block, (earn_rows, begin_at, span_len)), None

    zero_totals = (jnp.zeros((NT, num_states, num_states), jnp.float32), jnp.zeros((), jnp.float32), jnp.zeros((), jnp.float32))
    (counts, loglik, years), _ = lax.scan(accumulate, zero_totals, (earn_blocks, start_blocks, length_blocks, block_alive))
    weighted = probs * counts
    row_total = jnp.sum(weighted, axis=2, keepdims=True)
    factor = float(num_states * num_states * NT) / years
    trans_grad = factor * (weighted - probs * row_total)
    mean_loglik = jnp.reshape(loglik / years, (1,))
    return trans_grad, mean_loglik
```

```python
import functools

import jax
import jax.numpy as jnp
from jax import lax
from jax.sharding import PartitionSpec as P
from jax.experimental import pallas as pl
from jax.experimental.pallas import tpu as pltpu

HB = 128


top_precision = lax.Precision.HIGHEST


def emission(column, state_mean, log_sd):
    z_score = (column[:, None] - state_mean[None, :]) / jnp.exp(log_sd)[None, :]
    return jnp.exp(-0.5 * z_score * z_score - log_sd[None, :])


def per_device(
    earnings, starts, lengths, block_count, trans_logits, init_logits, state_mean, log_sd
):
    num_states = init_logits.shape[0]
    num_periods = earnings.shape[1]
    slot_rows = earnings.shape[0]
    group_size = lax.axis_size(("hh", "per"))
    core_count = lax.axis_size("st")
    half_states = num_states // core_count
    lead_state = lax.axis_index("st") * half_states
    whole_logits = lax.all_gather(trans_logits, ("per", "st"), axis=0, tiled=True)
    raised = jnp.exp(whole_logits.astype(jnp.float32))
    trans_probs = raised / jnp.sum(raised, axis=2, keepdims=True)
    raised_first = jnp.exp(init_logits)
    first_probs = raised_first / jnp.sum(raised_first)
    source_rows = slot_rows // group_size
    count_out = jnp.broadcast_to(block_count.reshape(1, 1), (1, group_size))
    got_earn, got_start, got_len, got_count = (
        lax.all_to_all(
            earnings.reshape(source_rows, group_size, num_periods),
            ("hh", "per"),
            split_axis=1,
            concat_axis=1,
            tiled=True,
        ),
        lax.all_to_all(
            starts.reshape(source_rows, group_size),
            ("hh", "per"),
            split_axis=1,
            concat_axis=1,
            tiled=True,
        ),
        lax.all_to_all(
            lengths.reshape(source_rows, group_size),
            ("hh", "per"),
            split_axis=1,
            concat_axis=1,
            tiled=True,
        ),
        lax.all_to_all(count_out, ("hh", "per"), split_axis=1, concat_axis=1, tiled=True),
    )
    per_source = got_count[0] * (HB // group_size)
    ends_at = jnp.cumsum(per_source)
    target_ids = jnp.arange(HB, dtype=jnp.int32)
    before_mask = ends_at[None, :] <= target_ids[:, None]
    source_ids = jnp.sum(before_mask.astype(jnp.int32), axis=1)
    begins_at = jnp.sum(jnp.where(before_mask, per_source[None, :], 0), axis=1)
    pick_ids = (target_ids - begins_at) * group_size + source_ids
    rows_earn = jnp.take(got_earn.reshape(source_rows * group_size, num_periods), pick_ids, axis=0)
    rows_start = jnp.take(got_start.reshape(source_rows * group_size), pick_ids)
    rows_len = jnp.take(got_len.reshape(source_rows * group_size), pick_ids)
    row_live = jnp.ones((HB,), dtype=bool)
    years_local = jnp.sum(jnp.where(row_live, rows_len, 0)).astype(jnp.float32)
    row_total_count = rows_earn.shape[0]
    columns = rows_earn.T
    period_ids = jnp.arange(num_periods, dtype=jnp.int32)

    def observed(step_now):
        return row_live & (step_now >= rows_start) & (step_now < rows_start + rows_len)

    def forward(prev_alpha, inputs):
        matrix, column, step_now = inputs
        fresh_start = (step_now <= rows_start)[:, None]
        moved_mass = jnp.dot(
            prev_alpha, matrix, precision=top_precision, preferred_element_type=jnp.float32
        )
        joint_mass = jnp.where(fresh_start, first_probs[None, :], moved_mass) * emission(
            column, state_mean, log_sd
        )
        seen_now = observed(step_now)
        scale_now = jnp.where(seen_now, jnp.sum(joint_mass, axis=1), 1.0)
        new_alpha = jnp.where(seen_now[:, None], joint_mass / scale_now[:, None], prev_alpha)
        return (new_alpha, (new_alpha, scale_now))

    start_alpha = jnp.broadcast_to(first_probs[None, :], (row_total_count, num_states))
    _, (alphas, scales) = lax.scan(forward, start_alpha, (trans_probs, columns, period_ids))

    def carry_of(back_now, column, scale_now, step_now):
        seen_now = observed(step_now)
        return jnp.where(
            seen_now[:, None],
            emission(column, state_mean, log_sd) * back_now / scale_now[:, None],
            0.0,
        )

    def backward(carry_now, inputs):
        matrix, alpha_prev, column_prev, scale_prev, step_now = inputs
        moving = row_live & (step_now > rows_start) & (step_now < rows_start + rows_len)
        weights = jnp.where(moving[:, None], alpha_prev, 0.0)
        own_carry = lax.dynamic_slice_in_dim(carry_now, lead_state, half_states, 1)
        grad_term = lax.dot_general(
            weights,
            own_carry,
            (((0,), (0,)), ((), ())),
            precision=top_precision,
            preferred_element_type=jnp.float32,
        )
        pulled = lax.dot_general(
            carry_now,
            matrix,
            (((1,), (1,)), ((), ())),
            precision=top_precision,
            preferred_element_type=jnp.float32,
        )
        back_now = jnp.where(moving[:, None], pulled, 1.0)
        return (carry_of(back_now, column_prev, scale_prev, step_now - 1), grad_term)

    ones_back = jnp.ones((row_total_count, num_states), jnp.float32)
    last_carry = carry_of(
        ones_back, columns[num_periods - 1], scales[num_periods - 1], num_periods - 1
    )
    _, grad_terms = lax.scan(
        backward,
        last_carry,
        (trans_probs[1:], alphas[:-1], columns[:-1], scales[:-1], period_ids[1:]),
        reverse=True,
    )
    zero_first = jnp.zeros((1,) + grad_terms.shape[1:], jnp.float32)
    partial_counts = jnp.concatenate([zero_first, grad_terms], axis=0)
    loglik_local = jnp.sum(jnp.log(scales))
    summed = lax.psum_scatter(partial_counts, "hh", scatter_dimension=1, tiled=True)
    summed = lax.psum_scatter(summed, "per", scatter_dimension=0, tiled=True)
    loglik_share = loglik_local / core_count
    years_share = years_local / core_count
    period_block = summed.shape[0]
    row_block_size = summed.shape[1]
    local_probs = lax.dynamic_slice(
        trans_probs,
        (lax.axis_index("per") * period_block, lax.axis_index("hh") * row_block_size, lead_state),
        (period_block, row_block_size, half_states),
    )
    weighted = local_probs * summed
    row_total, loglik_core, years_core = lax.psum(
        (jnp.sum(weighted, axis=2), loglik_share, years_share), "st"
    )
    loglik_all, years_all = lax.psum((loglik_core, years_core), ("hh", "per"))
    factor = float(num_states * num_states * num_periods) / years_all
    trans_grad = factor * (weighted - local_probs * row_total[:, :, None])
    mean_loglik = jnp.reshape(loglik_all / years_all, (1,))
    return (trans_grad, mean_loglik)


F32 = jnp.float32
BF = jnp.bfloat16
MESH = pl.DeviceIdType.MESH


def split_hi_lo(v):
    hi = v.astype(BF)
    return hi, (v - hi.astype(F32)).astype(BF)


def dot3(a, hi, lo, dims):
    ah, al = split_hi_lo(a)
    dd = lambda p, q: lax.dot_general(p, q, (dims, ((), ())), preferred_element_type=F32)
    return dd(ah, hi) + (dd(al, hi) + dd(ah, lo))


def fused_kernel(cfg, pack, logits, par, out, llout,
                 lg, got, amem, bmem, xsend, xrecv, aown, apart, uown, upart,
                 cbuf, zrecv, llbox, rts, rtr,
                 gsend, grecv, lrecv, lsend_p, lsend_x, lsend_r,
                 xs_sem, xr_sem, as_sem, ar_sem, us_sem, ur_sem,
                 zs_sem, zr_sem, lls_sem, llr_sem, rs_sem, rr_sem):
    nz, nt, half_t, own_t, rows, num_states = cfg
    x = lax.axis_index("per")
    z = lax.axis_index("hh")
    s = lax.axis_index("st")
    half = num_states // 2
    nsrc = nz * 2
    zr = num_states // nz
    slab = pack.shape[1]

    def rcopy(src, dst, ss, rs, dev):
        return pltpu.make_async_remote_copy(
            src_ref=src, dst_ref=dst, send_sem=ss, recv_sem=rs,
            device_id=dev, device_id_type=MESH)

    def arrived(ref, sem):
        pltpu.make_async_copy(ref, ref, sem).wait()

    barrier = pltpu.get_barrier_semaphore()
    others = []
    for dz in range(nz):
        for dx in range(2):
            for ds in range(2):
                if dz or dx or ds:
                    others.append({"hh": lax.rem(z + dz, nz), "per": lax.rem(x + dx, 2), "st": lax.rem(s + ds, 2)})
    for dev in others:
        pl.semaphore_signal(barrier, inc=1, device_id=dev, device_id_type=MESH)
    pl.semaphore_wait(barrier, len(others))

    partner = {"hh": z, "per": x, "st": 1 - s}
    across = {"hh": z, "per": 1 - x, "st": s}

    me_src = z * 2 + x
    hist = []
    n = 0
    for dz in range(nz):
        for dx in range(2):
            tz, tx = lax.rem(z + dz, nz), lax.rem(x + dx, 2)
            if dz == 0 and dx == 0:
                c = pltpu.make_async_copy(pack.at[tz * 2 + s], got.at[me_src], grecv.at[0])
            else:
                c = rcopy(pack.at[tz * 2 + s], got.at[me_src], gsend.at[n], grecv.at[n],
                          {"hh": tz, "per": tx, "st": s})
            c.start()
            hist.append(c)
            n += 1

    mine = own_t * (2 * x + s)
    sends = []
    for i in range(own_t):
        off = jnp.where(x == 0, own_t - 1 - i, i)
        near = own_t - 1 - off
        p = mine + near
        c = rcopy(logits.at[near], lg.at[p], lsend_p.at[i], lrecv.at[p], partner)
        c.start()
        sends.append(c)
        c = pltpu.make_async_copy(logits.at[near], lg.at[p], lrecv.at[p])
        c.start()
    for i in range(own_t):
        off = jnp.where(x == 0, own_t - 1 - i, i)
        p = mine + off
        c = rcopy(logits.at[off], lg.at[p], lsend_x.at[i], lrecv.at[p], across)
        c.start()
        sends.append(c)

    init = par[0:1, :]
    mean = par[1:2, :]
    log_sd = par[2:3, :]
    raised_first = jnp.exp(init)
    first = raised_first / jnp.sum(raised_first, axis=1, keepdims=True)
    inv_sd = jnp.exp(-log_sd)

    for n in range(nsrc):
        if n == 0:
            hist[0].wait()
        else:
            hist[n].wait_recv()
    base = jnp.zeros((1, 1), F32)
    years = jnp.zeros((1, 1), F32)
    picked = jnp.zeros((rows, 128), F32)
    lane = lax.broadcasted_iota(jnp.int32, (slab, rows), 1).astype(F32)
    sub = lax.broadcasted_iota(jnp.int32, (slab, rows), 0).astype(F32)
    for src in range(nsrc):
        g = got[src]
        live = g[0:1, nt + 2:nt + 3] * float(rows // nsrc)
        years = years + g[0:1, nt + 3:nt + 4]
        onehot = jnp.where((sub + base == lane) & (sub < live), 1.0, 0.0)
        picked = picked + lax.dot_general(
            onehot, g, (((0,), (0,)), ((), ())),
            precision=lax.Precision.HIGHEST, preferred_element_type=F32)
        base = base + live
    start = picked[:, nt:nt + 1]
    stop = start + picked[:, nt + 1:nt + 2]

    def emit(t):
        zs = (picked[:, t:t + 1] - mean) * inv_sd
        return jnp.exp(-0.5 * zs * zs - log_sd)

    def probs(t):
        r = jnp.exp(lg[t].astype(F32))
        return split_hi_lo(r / jnp.sum(r, axis=1, keepdims=True))

    def halves(ref, k, v):
        ref[k, 0] = v[:, :half]
        ref[k, 1] = v[:, half:]

    def whole(ref, k):
        return jnp.concatenate([ref[k, 0], ref[k, 1]], axis=1)

    def relay(i, xs):
        q = own_t * (2 * (1 - xs) + s) + (i if xs == 0 else own_t - 1 - i)
        arrived(lg.at[q], lrecv.at[q])
        c = rcopy(lg.at[q], lg.at[q], lsend_r.at[i], lrecv.at[q], partner)
        c.start()

    def need(t, xs):
        if (t // half_t) == xs:
            arrived(lg.at[t], lrecv.at[t])
        else:
            @pl.when(t // own_t != 2 * (1 - xs) + s)
            def _():
                arrived(lg.at[t], lrecv.at[t])

    def send_across(k, v):
        halves(xsend, k, v.astype(BF))
        rcopy(xsend.at[k], xrecv.at[k], xs_sem.at[k], xr_sem.at[k], across).start()

    def moving(t):
        return (float(t) > start) & (float(t) < stop)

    def stage_one(k, xs):
        arrived(xrecv.at[k], xr_sem.at[k])
        q = xs * half_t + k
        zsum = jnp.sum(whole(xrecv, k).astype(F32) * bmem[k], axis=1, keepdims=True)
        weight = jnp.where(moving(q), 1.0 / jnp.where(moving(q), zsum, 1.0), 0.0)
        scaled = (amem[k] * weight).astype(BF)
        if xs == 0:
            halves(aown, k, scaled)
            rcopy(aown.at[k], apart.at[k], as_sem.at[k], ar_sem.at[k], partner).start()
            rcopy(xrecv.at[k, 1 - s], upart.at[k], us_sem.at[k], ur_sem.at[k], partner).start()
        else:
            halves(uown, k, scaled)
            rcopy(xrecv.at[k], apart.at[k], as_sem.at[k], ar_sem.at[k], partner).start()
            rcopy(uown.at[k, 1 - s], upart.at[k], us_sem.at[k], ur_sem.at[k], partner).start()

    def stage_two(k, xs):
        arrived(apart.at[k], ar_sem.at[k])
        arrived(upart.at[k], ur_sem.at[k])
        a_ref, u_ref = (aown, xrecv) if xs == 0 else (xrecv, uown)
        u_all = jnp.concatenate([u_ref[k, s], upart[k]], axis=0)
        for b in range(2):
            a_all = jnp.concatenate([a_ref[k, b], apart[k, b]], axis=0)
            cbuf[k, b * half:(b + 1) * half, :] = lax.dot_general(
                a_all, u_all, (((0,), (0,)), ((), ())), preferred_element_type=F32)
        for dz in range(1, nz):
            tz = lax.rem(z + dz, nz)
            rcopy(cbuf.at[k, pl.ds(pl.multiple_of(tz * zr, 8), zr)], zrecv.at[dz - 1, k],
                  zs_sem.at[dz - 1, k], zr_sem.at[dz - 1, k],
                  {"hh": tz, "per": x, "st": s}).start()

    relay_at = {2: 0, 4: 1, 6: 2, 8: 3}

    @pl.when(x == 0)
    def _forward():
        todo = list(range(half_t - 1, 0, -1))
        ready = []
        total = jnp.zeros((rows, 1), F32)
        joint = scale_inv = None
        for t in range(nt):
            if t in relay_at:
                relay(relay_at[t], 0)
            e = emit(t)
            if t == 0:
                need(0, 0)
                joint = first * e
            else:
                need(t, 0)
                hi, lo = probs(t)
                moved = dot3(joint, hi, lo, ((1,), (0,))) * scale_inv
                if t < half_t:
                    bmem[t] = moved
                joint = jnp.where(float(t) <= start, first, moved) * e
            scale = jnp.sum(joint, axis=1, keepdims=True)
            seen = (float(t) >= start) & (float(t) < stop)
            total = total + jnp.where(seen, jnp.log(scale), 0.0)
            scale_inv = 1.0 / scale
            if t < half_t - 1:
                amem[t + 1] = joint * scale_inv
            elif t < nt - 1:
                send_across(t - (half_t - 1), joint * scale_inv)
            if t >= half_t + 1:
                if ready:
                    stage_two(ready.pop(0), 0)
                if todo:
                    k = todo.pop(0)
                    stage_one(k, 0)
                    ready.append(k)
        llsum = jnp.sum(total, axis=0, keepdims=True)
        llbox[z * 2 + s] = jnp.broadcast_to(llsum, (8, 128))
        for j, dev in enumerate(others):
            rcopy(llbox.at[z * 2 + s], llbox.at[z * 2 + s], lls_sem.at[j], llr_sem.at[z * 2 + s], dev).start()
        while todo or ready:
            if ready:
                stage_two(ready.pop(0), 0)
            if todo:
                k = todo.pop(0)
                stage_one(k, 0)
                ready.append(k)
        for j, dev in enumerate(others):
            rcopy(llbox.at[z * 2 + s], llbox.at[z * 2 + s], lls_sem.at[j], llr_sem.at[z * 2 + s], dev).wait_send()

    @pl.when(x == 1)
    def _backward():
        todo = list(range(half_t))
        ready = []
        back = jnp.ones((rows, num_states), F32)
        for step in range(nt - 1):
            t = nt - 1 - step
            if step in relay_at:
                relay(relay_at[step], 1)
            need(t, 1)
            hi, lo = probs(t)
            v = emit(t) * back
            norm_inv = 1.0 / jnp.sum(v, axis=1, keepdims=True)
            mv = moving(t)
            u = jnp.where(mv, v * norm_inv, 0.0)
            if t >= half_t:
                amem[t - half_t] = u
            else:
                send_across(t, u)
            if t > 1:
                back = jnp.where(mv, dot3(v, hi, lo, ((1,), (1,))) * norm_inv, 1.0)
                if t >= half_t:
                    bmem[t - half_t] = back
            if step >= half_t + 1:
                if ready:
                    stage_two(ready.pop(0), 1)
                if todo:
                    k = todo.pop(0)
                    stage_one(k, 1)
                    ready.append(k)
        need(0, 1)
        while todo or ready:
            if ready:
                stage_two(ready.pop(0), 1)
            if todo:
                k = todo.pop(0)
                stage_one(k, 1)
                ready.append(k)

    zrow = pl.ds(pl.multiple_of(z * zr, 8), zr)
    col = pl.ds(pl.multiple_of(s * half, 128), half)
    lane_out = lax.broadcasted_iota(jnp.int32, (zr, 128), 1)
    sums = jnp.zeros((zr, 128), F32)

    def slot(k, carry):
        q = x * half_t + k

        @pl.when(q > 0)
        def _():
            for d in range(nz - 1):
                arrived(zrecv.at[d, k], zr_sem.at[d, k])
            c = cbuf[k, zrow, :]
            for d in range(nz - 1):
                c = c + zrecv[d, k]
            r = jnp.exp(lg[q, zrow, :].astype(F32))
            mine_r = jnp.exp(lg[q, zrow, col].astype(F32))
            bmem[k, 0:zr, 0:half] = mine_r / jnp.sum(r, axis=1, keepdims=True)
            out[k] = bmem[k, 0:zr, 0:half] * c

        @pl.when(q == 0)
        def _():
            bmem[k, 0:zr, 0:half] = jnp.zeros((zr, half), F32)
            out[k] = jnp.zeros((zr, half), F32)
        row = jnp.sum(out[k], axis=1, keepdims=True)
        return carry + jnp.where(lane_out == k, row, 0.0)

    sums = lax.fori_loop(0, half_t, slot, sums)
    rts[...] = sums
    rc = rcopy(rts, rtr, rs_sem.at[0], rr_sem.at[0], partner)
    rc.start()

    for src in range(nsrc):
        @pl.when((x == 1) | (z * 2 + s != src))
        def _():
            arrived(llbox.at[src], llr_sem.at[src])
    ll = llbox[0, 0:1, :]
    for src in range(1, nsrc):
        ll = ll + llbox[src, 0:1, :]
    llout[...] = ll / years
    factor = float(num_states * num_states * nt) / years
    rc.wait()
    rtot = rts[...] + rtr[...]
    for k in range(half_t):
        out[k] = factor * (out[k] - bmem[k, 0:zr, 0:half] * rtot[:, k:k + 1])

    for n in range(1, nsrc):
        hist[n].wait_send()
    for c in sends:
        c.wait_send()
    for i in range(own_t):
        rcopy(lg.at[0], lg.at[0], lsend_r.at[i], lrecv.at[0], partner).wait_send()
    for k in range(half_t):
        def drain(k=k):
            rcopy(aown.at[k], apart.at[k], as_sem.at[k], ar_sem.at[k], partner).wait_send()
            rcopy(uown.at[k, 0], upart.at[k], us_sem.at[k], ur_sem.at[k], partner).wait_send()
            for d in range(nz - 1):
                rcopy(cbuf.at[k, pl.ds(0, zr)], zrecv.at[d, k], zs_sem.at[d, k], zr_sem.at[d, k], partner).wait_send()
        if k == 0:
            pl.when(x == 1)(drain)
            @pl.when(x == 0)
            def _():
                rcopy(xsend.at[0], xrecv.at[0], xs_sem.at[0], xr_sem.at[0], across).wait_send()
        else:
            drain()
            rcopy(xsend.at[k], xrecv.at[k], xs_sem.at[k], xr_sem.at[k], across).wait_send()


def fused_device(
    earnings, starts, lengths, block_count, trans_logits, init_logits, state_mean, log_sd
):
    num_states = init_logits.shape[0]
    nt = earnings.shape[1]
    slot_rows = earnings.shape[0]
    nz = lax.axis_size("hh")
    nsrc = nz * 2
    slab = slot_rows // nsrc
    own_t = trans_logits.shape[0]
    half_t = nt // 2
    half = num_states // 2
    zr = num_states // nz
    rows = HB
    count = block_count.astype(F32)[0]
    live = jnp.arange(slot_rows, dtype=jnp.int32) < block_count[0] * HB
    years = jnp.sum(jnp.where(live, lengths, 0)).astype(F32)
    pack = jnp.concatenate(
        [earnings, starts.astype(F32)[:, None], lengths.astype(F32)[:, None],
         jnp.broadcast_to(count, (slot_rows, 1)), jnp.broadcast_to(years, (slot_rows, 1)),
         jnp.zeros((slot_rows, 128 - nt - 4), F32)], axis=1)
    pack = pack.reshape(slab, nsrc, 128).transpose(1, 0, 2)
    par = jnp.concatenate(
        [init_logits[None], state_mean[None], log_sd[None], jnp.zeros((5, num_states), F32)], axis=0)
    cfg = (nz, nt, half_t, own_t, rows, num_states)
    V = pltpu.VMEM
    D = pltpu.SemaphoreType.DMA
    vm = pl.BlockSpec(memory_space=pltpu.VMEM)
    grad, ll = pl.pallas_call(
        functools.partial(fused_kernel, cfg),
        out_shape=(jax.ShapeDtypeStruct((half_t, zr, half), F32),
                   jax.ShapeDtypeStruct((1, 128), F32)),
        in_specs=[vm] * 3,
        out_specs=(vm, vm),
        scratch_shapes=[
            V((nt, num_states, num_states), BF),
            V((nsrc, slab, 128), F32),
            V((half_t, rows, num_states), F32),
            V((half_t, rows, num_states), F32),
            V((half_t, 2, rows, half), BF),
            V((half_t, 2, rows, half), BF),
            V((half_t, 2, rows, half), BF),
            V((half_t, 2, rows, half), BF),
            V((half_t, 2, rows, half), BF),
            V((half_t, rows, half), BF),
            V((half_t, num_states, half), F32),
            V((nz - 1, half_t, zr, half), F32),
            V((nsrc, 8, 128), F32),
            V((zr, 128), F32),
            V((zr, 128), F32),
            D((nsrc,)), D((nsrc,)), D((nt,)), D((own_t,)), D((own_t,)), D((own_t,)),
            D((half_t,)), D((half_t,)), D((half_t,)), D((half_t,)), D((half_t,)), D((half_t,)),
            D((nz - 1, half_t)), D((nz - 1, half_t)), D((4 * nz,)), D((nsrc,)), D((1,)), D((1,)),
        ],
        compiler_params=pltpu.CompilerParams(
            collective_id=0, has_side_effects=True, vmem_limit_bytes=56 * 1024 * 1024),
        name="chain",
    )(pack, trans_logits, par)
    return grad, ll[0, 0:1]


def solution(mesh):
    fits = mesh.shape["per"] == 2 and mesh.shape["st"] == 2 and HB % (mesh.shape["hh"] * 2) == 0
    body = fused_device if fits else per_device
    placed = (
        P(("hh", "per"), None),
        P(("hh", "per")),
        P(("hh", "per")),
        P(("hh", "per")),
        P(("grp", "per", "st"), None, None),
        P("grp"),
        P("grp"),
        P("grp"),
    )
    return jax.shard_map(
        body,
        mesh=mesh,
        in_specs=placed,
        out_specs=(P(("grp", "per"), "hh", "st"), P("grp")),
        check_vma=False,
    )
```

```python
import functools

import jax
import jax.numpy as jnp
from jax import lax
from jax.sharding import PartitionSpec as P
from jax.experimental import pallas as pl
from jax.experimental.pallas import tpu as pltpu

HB = 128


top_precision = lax.Precision.HIGHEST


def emission(column, state_mean, log_sd):
    z_score = (column[:, None] - state_mean[None, :]) / jnp.exp(log_sd)[None, :]
    return jnp.exp(-0.5 * z_score * z_score - log_sd[None, :])


def per_device(
    earnings, starts, lengths, block_count, trans_logits, init_logits, state_mean, log_sd
):
    num_states = init_logits.shape[0]
    num_periods = earnings.shape[1]
    slot_rows = earnings.shape[0]
    group_size = lax.axis_size(("hh", "per"))
    core_count = lax.axis_size("st")
    half_states = num_states // core_count
    lead_state = lax.axis_index("st") * half_states
    whole_logits = lax.all_gather(trans_logits, ("per", "st"), axis=0, tiled=True)
    raised = jnp.exp(whole_logits.astype(jnp.float32))
    trans_probs = raised / jnp.sum(raised, axis=2, keepdims=True)
    raised_first = jnp.exp(init_logits)
    first_probs = raised_first / jnp.sum(raised_first)
    source_rows = slot_rows // group_size
    count_out = jnp.broadcast_to(block_count.reshape(1, 1), (1, group_size))
    got_earn, got_start, got_len, got_count = (
        lax.all_to_all(
            earnings.reshape(source_rows, group_size, num_periods),
            ("hh", "per"),
            split_axis=1,
            concat_axis=1,
            tiled=True,
        ),
        lax.all_to_all(
            starts.reshape(source_rows, group_size),
            ("hh", "per"),
            split_axis=1,
            concat_axis=1,
            tiled=True,
        ),
        lax.all_to_all(
            lengths.reshape(source_rows, group_size),
            ("hh", "per"),
            split_axis=1,
            concat_axis=1,
            tiled=True,
        ),
        lax.all_to_all(count_out, ("hh", "per"), split_axis=1, concat_axis=1, tiled=True),
    )
    per_source = got_count[0] * (HB // group_size)
    ends_at = jnp.cumsum(per_source)
    target_ids = jnp.arange(HB, dtype=jnp.int32)
    before_mask = ends_at[None, :] <= target_ids[:, None]
    source_ids = jnp.sum(before_mask.astype(jnp.int32), axis=1)
    begins_at = jnp.sum(jnp.where(before_mask, per_source[None, :], 0), axis=1)
    pick_ids = (target_ids - begins_at) * group_size + source_ids
    rows_earn = jnp.take(got_earn.reshape(source_rows * group_size, num_periods), pick_ids, axis=0)
    rows_start = jnp.take(got_start.reshape(source_rows * group_size), pick_ids)
    rows_len = jnp.take(got_len.reshape(source_rows * group_size), pick_ids)
    row_live = jnp.ones((HB,), dtype=bool)
    years_local = jnp.sum(jnp.where(row_live, rows_len, 0)).astype(jnp.float32)
    row_total_count = rows_earn.shape[0]
    columns = rows_earn.T
    period_ids = jnp.arange(num_periods, dtype=jnp.int32)

    def observed(step_now):
        return row_live & (step_now >= rows_start) & (step_now < rows_start + rows_len)

    def forward(prev_alpha, inputs):
        matrix, column, step_now = inputs
        fresh_start = (step_now <= rows_start)[:, None]
        moved_mass = jnp.dot(
            prev_alpha, matrix, precision=top_precision, preferred_element_type=jnp.float32
        )
        joint_mass = jnp.where(fresh_start, first_probs[None, :], moved_mass) * emission(
            column, state_mean, log_sd
        )
        seen_now = observed(step_now)
        scale_now = jnp.where(seen_now, jnp.sum(joint_mass, axis=1), 1.0)
        new_alpha = jnp.where(seen_now[:, None], joint_mass / scale_now[:, None], prev_alpha)
        return (new_alpha, (new_alpha, scale_now))

    start_alpha = jnp.broadcast_to(first_probs[None, :], (row_total_count, num_states))
    _, (alphas, scales) = lax.scan(forward, start_alpha, (trans_probs, columns, period_ids))

    def carry_of(back_now, column, scale_now, step_now):
        seen_now = observed(step_now)
        return jnp.where(
            seen_now[:, None],
            emission(column, state_mean, log_sd) * back_now / scale_now[:, None],
            0.0,
        )

    def backward(carry_now, inputs):
        matrix, alpha_prev, column_prev, scale_prev, step_now = inputs
        moving = row_live & (step_now > rows_start) & (step_now < rows_start + rows_len)
        weights = jnp.where(moving[:, None], alpha_prev, 0.0)
        own_carry = lax.dynamic_slice_in_dim(carry_now, lead_state, half_states, 1)
        grad_term = lax.dot_general(
            weights,
            own_carry,
            (((0,), (0,)), ((), ())),
            precision=top_precision,
            preferred_element_type=jnp.float32,
        )
        pulled = lax.dot_general(
            carry_now,
            matrix,
            (((1,), (1,)), ((), ())),
            precision=top_precision,
            preferred_element_type=jnp.float32,
        )
        back_now = jnp.where(moving[:, None], pulled, 1.0)
        return (carry_of(back_now, column_prev, scale_prev, step_now - 1), grad_term)

    ones_back = jnp.ones((row_total_count, num_states), jnp.float32)
    last_carry = carry_of(
        ones_back, columns[num_periods - 1], scales[num_periods - 1], num_periods - 1
    )
    _, grad_terms = lax.scan(
        backward,
        last_carry,
        (trans_probs[1:], alphas[:-1], columns[:-1], scales[:-1], period_ids[1:]),
        reverse=True,
    )
    zero_first = jnp.zeros((1,) + grad_terms.shape[1:], jnp.float32)
    partial_counts = jnp.concatenate([zero_first, grad_terms], axis=0)
    loglik_local = jnp.sum(jnp.log(scales))
    summed = lax.psum_scatter(partial_counts, "hh", scatter_dimension=1, tiled=True)
    summed = lax.psum_scatter(summed, "per", scatter_dimension=0, tiled=True)
    loglik_share = loglik_local / core_count
    years_share = years_local / core_count
    period_block = summed.shape[0]
    row_block_size = summed.shape[1]
    local_probs = lax.dynamic_slice(
        trans_probs,
        (lax.axis_index("per") * period_block, lax.axis_index("hh") * row_block_size, lead_state),
        (period_block, row_block_size, half_states),
    )
    weighted = local_probs * summed
    row_total, loglik_core, years_core = lax.psum(
        (jnp.sum(weighted, axis=2), loglik_share, years_share), "st"
    )
    loglik_all, years_all = lax.psum((loglik_core, years_core), ("hh", "per"))
    factor = float(num_states * num_states * num_periods) / years_all
    trans_grad = factor * (weighted - local_probs * row_total[:, :, None])
    mean_loglik = jnp.reshape(loglik_all / years_all, (1,))
    return (trans_grad, mean_loglik)


F32 = jnp.float32
BF = jnp.bfloat16
MESH = pl.DeviceIdType.MESH


def split_hi_lo(v):
    hi = v.astype(BF)
    return hi, (v - hi.astype(F32)).astype(BF)


def dot3(a, hi, lo, dims):
    ah, al = split_hi_lo(a)
    dd = lambda p, q: lax.dot_general(p, q, (dims, ((), ())), preferred_element_type=F32)
    return dd(ah, hi) + (dd(al, hi) + dd(ah, lo))


def three_way(v):
    hi = v.astype(BF)
    rest = v - hi.astype(F32)
    mid = rest.astype(BF)
    return hi, mid, (rest - mid.astype(F32)).astype(BF)


def sum3(pieces, right, dims):
    dd = lambda p: lax.dot_general(p, right, (dims, ((), ())), preferred_element_type=F32)
    return (dd(pieces[0]) + dd(pieces[1])) + dd(pieces[2])


def fused_kernel(cfg, earn, begin, length, count, logits, init_ref, mean_ref, sd_ref, out, llout,
                 pack, lg, got, amem, bmem, xsend, xrecv, aown, apart, uown, upart,
                 cbuf, zrecv, zmid, zfar, llbox, rts, rtr,
                 gsend, grecv, lrecv, lsend_p, lsend_x, lsend_r,
                 xs_sem, xr_sem, as_sem, ar_sem, us_sem, ur_sem,
                 zs_sem, zr_sem, zfs_sem, zfr_sem, lls_sem, llr_sem, rs_sem, rr_sem):
    nz, nt, half_t, own_t, rows, num_states = cfg
    x = lax.axis_index("per")
    z = lax.axis_index("hh")
    s = lax.axis_index("st")
    half = num_states // 2
    nsrc = nz * 2
    zr = num_states // nz
    slots = earn.shape[1]
    slab = slots // nsrc

    def rcopy(src, dst, ss, rs, dev):
        return pltpu.make_async_remote_copy(
            src_ref=src, dst_ref=dst, send_sem=ss, recv_sem=rs,
            device_id=dev, device_id_type=MESH)

    def arrived(ref, sem):
        pltpu.make_async_copy(ref, ref, sem).wait()

    barrier = pltpu.get_barrier_semaphore()
    others = []
    for dz in range(nz):
        for dx in range(2):
            for ds in range(2):
                if dz or dx or ds:
                    others.append({"hh": lax.rem(z + dz, nz), "per": lax.rem(x + dx, 2), "st": lax.rem(s + ds, 2)})
    for dev in others:
        pl.semaphore_signal(barrier, inc=1, device_id=dev, device_id_type=MESH)

    cnt = count[0].astype(F32)
    spot = lax.broadcasted_iota(jnp.int32, (1, slots), 1).astype(F32)
    lens = length[...].astype(F32)
    own_years = jnp.sum(jnp.where(spot < cnt * float(rows), lens, 0.0), axis=1, keepdims=True)
    table = jnp.concatenate(
        [earn[...], begin[...].astype(F32), lens, jnp.full((1, slots), 1.0, F32) * cnt,
         jnp.broadcast_to(own_years, (1, slots)), jnp.zeros((4, slots), F32)], axis=0)
    pieces = three_way(table)
    q_id = lax.broadcasted_iota(jnp.int32, (slots, 128), 0)
    r_id = lax.broadcasted_iota(jnp.int32, (slots, 128), 1)
    for tz in range(nz):
        pick = jnp.where((q_id == r_id * nsrc + (tz * 2 + s)) & (r_id < slab), 1.0, 0.0).astype(BF)
        pack[tz] = sum3(pieces, pick, ((1,), (0,)))
    pl.semaphore_wait(barrier, len(others))

    partner = {"hh": z, "per": x, "st": 1 - s}
    across = {"hh": z, "per": 1 - x, "st": s}
    near_z = z + 1 - 2 * lax.rem(z, 2)
    near_par = lax.rem(near_z, 2)
    far_z = lax.rem(z + 2, 4)
    near = {"hh": near_z, "per": x, "st": s}
    far = {"hh": far_z, "per": x, "st": s}

    me_src = z * 2 + x
    hist = []
    n = 0
    for dz in range(nz):
        for dx in range(2):
            tz, tx = lax.rem(z + dz, nz), lax.rem(x + dx, 2)
            if dz == 0 and dx == 0:
                c = pltpu.make_async_copy(pack.at[tz], got.at[me_src], grecv.at[0])
            else:
                c = rcopy(pack.at[tz], got.at[me_src], gsend.at[n], grecv.at[n],
                          {"hh": tz, "per": tx, "st": s})
            c.start()
            hist.append(c)
            n += 1

    mine = own_t * (2 * x + s)
    sends = []
    for i in range(own_t):
        off = jnp.where(x == 0, own_t - 1 - i, i)
        back_off = own_t - 1 - off
        p = mine + back_off
        c = rcopy(logits.at[back_off], lg.at[p], lsend_p.at[i], lrecv.at[p], partner)
        c.start()
        sends.append(c)
        c = pltpu.make_async_copy(logits.at[back_off], lg.at[p], lrecv.at[p])
        c.start()
    for i in range(own_t):
        off = jnp.where(x == 0, own_t - 1 - i, i)
        p = mine + off
        c = rcopy(logits.at[off], lg.at[p], lsend_x.at[i], lrecv.at[p], across)
        c.start()
        sends.append(c)

    init = init_ref[...]
    mean = mean_ref[...]
    log_sd = sd_ref[...]
    raised_first = jnp.exp(init)
    first = raised_first / jnp.sum(raised_first, axis=1, keepdims=True)
    inv_sd = jnp.exp(-log_sd)

    for n in range(nsrc):
        if n == 0:
            hist[0].wait()
        else:
            hist[n].wait_recv()
    base = jnp.zeros((1, 1), F32)
    years = jnp.zeros((1, 1), F32)
    seat = lax.broadcasted_iota(jnp.int32, (rows, 128), 0).astype(F32)
    lane = lax.broadcasted_iota(jnp.int32, (rows, 128), 1).astype(F32)
    hots = []
    for src in range(nsrc):
        live = got[src, nt + 2:nt + 3, 0:1] * float(rows // nsrc)
        years = years + got[src, nt + 3:nt + 4, 0:1]
        hots.append(jnp.where((lane + base == seat) & (lane < live), 1.0, 0.0).astype(BF))
        base = base + live
    hot = jnp.concatenate(hots, axis=1)
    wide = jnp.concatenate([got[src] for src in range(nsrc)], axis=1)
    dd = lambda g: lax.dot_general(hot, g, (((1,), (1,)), ((), ())), preferred_element_type=F32)
    g0, g1, g2 = three_way(wide)
    picked = (dd(g0) + dd(g1)) + dd(g2)
    start = picked[:, nt:nt + 1]
    stop = start + picked[:, nt + 1:nt + 2]

    def emit(t):
        zs = (picked[:, t:t + 1] - mean) * inv_sd
        return jnp.exp(-0.5 * zs * zs - log_sd)

    def probs(t):
        r = jnp.exp(lg[t].astype(F32))
        return split_hi_lo(r / jnp.sum(r, axis=1, keepdims=True))

    def halves(ref, k, v):
        ref[k, 0] = v[:, :half]
        ref[k, 1] = v[:, half:]

    def whole(ref, k):
        return jnp.concatenate([ref[k, 0], ref[k, 1]], axis=1)

    def relay(i, xs):
        q = own_t * (2 * (1 - xs) + s) + (i if xs == 0 else own_t - 1 - i)
        arrived(lg.at[q], lrecv.at[q])
        c = rcopy(lg.at[q], lg.at[q], lsend_r.at[i], lrecv.at[q], partner)
        c.start()

    def need(t, xs):
        if (t // half_t) == xs:
            arrived(lg.at[t], lrecv.at[t])
        else:
            @pl.when(t // own_t != 2 * (1 - xs) + s)
            def _():
                arrived(lg.at[t], lrecv.at[t])

    def send_across(k, v):
        halves(xsend, k, v.astype(BF))
        rcopy(xsend.at[k], xrecv.at[k], xs_sem.at[k], xr_sem.at[k], across).start()

    def moving(t):
        return (float(t) > start) & (float(t) < stop)

    def stage_one(k, xs):
        arrived(xrecv.at[k], xr_sem.at[k])
        q = xs * half_t + k
        zsum = jnp.sum(whole(xrecv, k).astype(F32) * bmem[k], axis=1, keepdims=True)
        weight = jnp.where(moving(q), 1.0 / jnp.where(moving(q), zsum, 1.0), 0.0)
        scaled = (amem[k] * weight).astype(BF)
        if xs == 0:
            halves(aown, k, scaled)
            rcopy(aown.at[k], apart.at[k], as_sem.at[k], ar_sem.at[k], partner).start()
            rcopy(xrecv.at[k, 1 - s], upart.at[k], us_sem.at[k], ur_sem.at[k], partner).start()
        else:
            halves(uown, k, scaled)
            rcopy(xrecv.at[k], apart.at[k], as_sem.at[k], ar_sem.at[k], partner).start()
            rcopy(uown.at[k, 1 - s], upart.at[k], us_sem.at[k], ur_sem.at[k], partner).start()

    def stage_two(k, xs):
        arrived(apart.at[k], ar_sem.at[k])
        arrived(upart.at[k], ur_sem.at[k])
        a_ref, u_ref = (aown, xrecv) if xs == 0 else (xrecv, uown)
        u_all = jnp.concatenate([u_ref[k, s], upart[k]], axis=0)
        for b in range(2):
            a_all = jnp.concatenate([a_ref[k, b], apart[k, b]], axis=0)
            cbuf[k, b * half:(b + 1) * half, :] = lax.dot_general(
                a_all, u_all, (((0,), (0,)), ((), ())), preferred_element_type=F32)
        for j in range(2):
            rcopy(cbuf.at[k, pl.ds(pl.multiple_of((near_par + 2 * j) * zr, 8), zr)], zrecv.at[j, k],
                  zs_sem.at[j, k], zr_sem.at[j, k], near).start()

    def stage_three(k):
        for j in range(2):
            arrived(zrecv.at[j, k], zr_sem.at[j, k])
        here, there = z // 2, 1 - z // 2
        zmid[k] = zrecv[here, k] + cbuf[k, pl.ds(pl.multiple_of(z * zr, 8), zr), :]
        cbuf[k, pl.ds(pl.multiple_of(far_z * zr, 8), zr), :] = (
            zrecv[there, k] + cbuf[k, pl.ds(pl.multiple_of(far_z * zr, 8), zr), :])
        rcopy(cbuf.at[k, pl.ds(pl.multiple_of(far_z * zr, 8), zr)], zfar.at[k],
              zfs_sem.at[k], zfr_sem.at[k], far).start()

    def advance(xs, todo, ready, summed):
        if len(summed) > 1 or (summed and not ready):
            stage_three(summed.pop(0))
        if ready:
            k = ready.pop(0)
            stage_two(k, xs)
            summed.append(k)
        if todo:
            k = todo.pop(0)
            stage_one(k, xs)
            ready.append(k)

    relay_at = {1: 0, 3: 1, 5: 2, 7: 3}

    @pl.when(x == 0)
    def _forward():
        todo = list(range(half_t - 1, 0, -1))
        ready, summed = [], []
        total = jnp.zeros((rows, 1), F32)
        joint = scale_inv = None
        for t in range(nt):
            if t in relay_at:
                relay(relay_at[t], 0)
            e = emit(t)
            if t == 0:
                need(0, 0)
                need(1, 0)
                joint = first * e
                hi, lo = probs(1)
            else:
                if t + 1 < nt:
                    need(t + 1, 0)
                    nxt = probs(t + 1)
                moved = dot3(joint, hi, lo, ((1,), (0,))) * scale_inv
                if t < half_t:
                    bmem[t] = moved
                joint = jnp.where(float(t) <= start, first, moved) * e
                if t + 1 < nt:
                    hi, lo = nxt
            scale = jnp.sum(joint, axis=1, keepdims=True)
            seen = (float(t) >= start) & (float(t) < stop)
            total = total + jnp.where(seen, jnp.log(scale), 0.0)
            scale_inv = 1.0 / scale
            if t < half_t - 1:
                amem[t + 1] = joint * scale_inv
            elif t < nt - 1:
                send_across(t - (half_t - 1), joint * scale_inv)
            if t >= half_t + 1:
                advance(0, todo, ready, summed)
        llsum = jnp.sum(total, axis=0, keepdims=True)
        llbox[z * 2 + s] = jnp.broadcast_to(llsum, (8, 128))
        for j, dev in enumerate(others):
            rcopy(llbox.at[z * 2 + s], llbox.at[z * 2 + s], lls_sem.at[j], llr_sem.at[z * 2 + s], dev).start()
        while todo or ready or summed:
            advance(0, todo, ready, summed)
        for j, dev in enumerate(others):
            rcopy(llbox.at[z * 2 + s], llbox.at[z * 2 + s], lls_sem.at[j], llr_sem.at[z * 2 + s], dev).wait_send()

    @pl.when(x == 1)
    def _backward():
        todo = list(range(half_t))
        ready, summed = [], []
        back = jnp.ones((rows, num_states), F32)
        for step in range(nt - 1):
            t = nt - 1 - step
            if step in relay_at:
                relay(relay_at[step], 1)
            if step == 0:
                need(t, 1)
                hi, lo = probs(t)
            if t > 2:
                need(t - 1, 1)
                nxt = probs(t - 1)
            v = emit(t) * back
            norm_inv = 1.0 / jnp.sum(v, axis=1, keepdims=True)
            mv = moving(t)
            u = jnp.where(mv, v * norm_inv, 0.0)
            if t >= half_t:
                amem[t - half_t] = u
            else:
                send_across(t, u)
            if t > 1:
                back = jnp.where(mv, dot3(v, hi, lo, ((1,), (1,))) * norm_inv, 1.0)
                if t >= half_t:
                    bmem[t - half_t] = back
                if t > 2:
                    hi, lo = nxt
            if step >= half_t + 1:
                advance(1, todo, ready, summed)
        need(1, 1)
        need(0, 1)
        while todo or ready or summed:
            advance(1, todo, ready, summed)

    zrow = pl.ds(pl.multiple_of(z * zr, 8), zr)
    col = pl.ds(pl.multiple_of(s * half, 128), half)
    lane_out = lax.broadcasted_iota(jnp.int32, (zr, 128), 1)
    sums = jnp.zeros((zr, 128), F32)

    def slot(k, carry):
        q = x * half_t + k

        @pl.when(q > 0)
        def _():
            arrived(zfar.at[k], zfr_sem.at[k])
            c = zmid[k] + zfar[k]
            r = jnp.exp(lg[q, zrow, :].astype(F32))
            mine_r = jnp.exp(lg[q, zrow, col].astype(F32))
            bmem[k, 0:zr, 0:half] = mine_r / jnp.sum(r, axis=1, keepdims=True)
            out[k] = bmem[k, 0:zr, 0:half] * c

        @pl.when(q == 0)
        def _():
            bmem[k, 0:zr, 0:half] = jnp.zeros((zr, half), F32)
            out[k] = jnp.zeros((zr, half), F32)
        row = jnp.sum(out[k], axis=1, keepdims=True)
        return carry + jnp.where(lane_out == k, row, 0.0)

    sums = lax.fori_loop(0, half_t, slot, sums)
    rts[...] = sums
    rc = rcopy(rts, rtr, rs_sem.at[0], rr_sem.at[0], partner)
    rc.start()

    for src in range(nsrc):
        @pl.when((x == 1) | (z * 2 + s != src))
        def _():
            arrived(llbox.at[src], llr_sem.at[src])
    ll = llbox[0, 0:1, :]
    for src in range(1, nsrc):
        ll = ll + llbox[src, 0:1, :]
    llout[...] = ll / years
    factor = float(num_states * num_states * nt) / years
    rc.wait()
    rtot = rts[...] + rtr[...]
    for k in range(half_t):
        out[k] = factor * (out[k] - bmem[k, 0:zr, 0:half] * rtot[:, k:k + 1])

    for n in range(1, nsrc):
        hist[n].wait_send()
    for c in sends:
        c.wait_send()
    for i in range(own_t):
        rcopy(lg.at[0], lg.at[0], lsend_r.at[i], lrecv.at[0], partner).wait_send()
    for k in range(half_t):
        def drain(k=k):
            rcopy(aown.at[k], apart.at[k], as_sem.at[k], ar_sem.at[k], partner).wait_send()
            rcopy(uown.at[k, 0], upart.at[k], us_sem.at[k], ur_sem.at[k], partner).wait_send()
            for d in range(2):
                rcopy(cbuf.at[k, pl.ds(0, zr)], zrecv.at[d, k], zs_sem.at[d, k], zr_sem.at[d, k], near).wait_send()
            rcopy(cbuf.at[k, pl.ds(0, zr)], zfar.at[k], zfs_sem.at[k], zfr_sem.at[k], far).wait_send()
        if k == 0:
            pl.when(x == 1)(drain)
            @pl.when(x == 0)
            def _():
                rcopy(xsend.at[0], xrecv.at[0], xs_sem.at[0], xr_sem.at[0], across).wait_send()
        else:
            drain()
            rcopy(xsend.at[k], xrecv.at[k], xs_sem.at[k], xr_sem.at[k], across).wait_send()


def fused_device(
    earnings, starts, lengths, block_count, trans_logits, init_logits, state_mean, log_sd
):
    num_states = init_logits.shape[0]
    nt = earnings.shape[1]
    slot_rows = earnings.shape[0]
    nz = lax.axis_size("hh")
    nsrc = nz * 2
    slab = slot_rows // nsrc
    own_t = trans_logits.shape[0]
    half_t = nt // 2
    half = num_states // 2
    zr = num_states // nz
    rows = HB
    cfg = (nz, nt, half_t, own_t, rows, num_states)
    V = pltpu.VMEM
    D = pltpu.SemaphoreType.DMA
    vm = pl.BlockSpec(memory_space=pltpu.VMEM)
    grad, ll = pl.pallas_call(
        functools.partial(fused_kernel, cfg),
        out_shape=(jax.ShapeDtypeStruct((half_t, zr, half), F32),
                   jax.ShapeDtypeStruct((1, 128), F32)),
        in_specs=[vm, vm, vm, pl.BlockSpec(memory_space=pltpu.SMEM), pl.BlockSpec(memory_space=pl.ANY), vm, vm, vm],
        out_specs=(vm, vm),
        scratch_shapes=[
            V((nz, nt + 8, 128), F32),
            V((nt, num_states, num_states), BF),
            V((nsrc, nt + 8, 128), F32),
            V((half_t, rows, num_states), F32),
            V((half_t, rows, num_states), F32),
            V((half_t, 2, rows, half), BF),
            V((half_t, 2, rows, half), BF),
            V((half_t, 2, rows, half), BF),
            V((half_t, 2, rows, half), BF),
            V((half_t, 2, rows, half), BF),
            V((half_t, rows, half), BF),
            V((half_t, num_states, half), F32),
            V((2, half_t, zr, half), F32),
            V((half_t, zr, half), F32),
            V((half_t, zr, half), F32),
            V((nsrc, 8, 128), F32),
            V((zr, 128), F32),
            V((zr, 128), F32),
            D((nsrc,)), D((nsrc,)), D((nt,)), D((own_t,)), D((own_t,)), D((own_t,)),
            D((half_t,)), D((half_t,)), D((half_t,)), D((half_t,)), D((half_t,)), D((half_t,)),
            D((2, half_t)), D((2, half_t)), D((half_t,)), D((half_t,)), D((4 * nz,)), D((nsrc,)), D((1,)), D((1,)),
        ],
        compiler_params=pltpu.CompilerParams(
            collective_id=0, has_side_effects=True, vmem_limit_bytes=56 * 1024 * 1024),
        name="chain",
    )(earnings.T, starts[None], lengths[None], block_count, trans_logits,
      init_logits[None], state_mean[None], log_sd[None])
    return grad, ll[0, 0:1]


def solution(mesh):
    fits = mesh.shape["per"] == 2 and mesh.shape["st"] == 2 and mesh.shape["hh"] == 4
    body = fused_device if fits else per_device
    placed = (
        P(("hh", "per"), None),
        P(("hh", "per")),
        P(("hh", "per")),
        P(("hh", "per")),
        P(("grp", "per", "st"), None, None),
        P("grp"),
        P("grp"),
        P("grp"),
    )
    return jax.shard_map(
        body,
        mesh=mesh,
        in_specs=placed,
        out_specs=(P(("grp", "per"), "hh", "st"), P("grp")),
        check_vma=False,
    )
```

```python
import functools

import jax
import jax.numpy as jnp
from jax import lax
from jax.sharding import PartitionSpec as P
from jax.experimental import pallas as pl
from jax.experimental.pallas import tpu as pltpu

HB = 128


top_precision = lax.Precision.HIGHEST


def emission(column, state_mean, log_sd):
    z_score = (column[:, None] - state_mean[None, :]) / jnp.exp(log_sd)[None, :]
    return jnp.exp(-0.5 * z_score * z_score - log_sd[None, :])


def per_device(
    earnings, starts, lengths, block_count, trans_logits, init_logits, state_mean, log_sd
):
    num_states = init_logits.shape[0]
    num_periods = earnings.shape[1]
    slot_rows = earnings.shape[0]
    group_size = lax.axis_size(("hh", "per"))
    core_count = lax.axis_size("st")
    half_states = num_states // core_count
    lead_state = lax.axis_index("st") * half_states
    whole_logits = lax.all_gather(trans_logits, ("per", "st"), axis=0, tiled=True)
    raised = jnp.exp(whole_logits.astype(jnp.float32))
    trans_probs = raised / jnp.sum(raised, axis=2, keepdims=True)
    raised_first = jnp.exp(init_logits)
    first_probs = raised_first / jnp.sum(raised_first)
    source_rows = slot_rows // group_size
    count_out = jnp.broadcast_to(block_count.reshape(1, 1), (1, group_size))
    got_earn, got_start, got_len, got_count = (
        lax.all_to_all(
            earnings.reshape(source_rows, group_size, num_periods),
            ("hh", "per"),
            split_axis=1,
            concat_axis=1,
            tiled=True,
        ),
        lax.all_to_all(
            starts.reshape(source_rows, group_size),
            ("hh", "per"),
            split_axis=1,
            concat_axis=1,
            tiled=True,
        ),
        lax.all_to_all(
            lengths.reshape(source_rows, group_size),
            ("hh", "per"),
            split_axis=1,
            concat_axis=1,
            tiled=True,
        ),
        lax.all_to_all(count_out, ("hh", "per"), split_axis=1, concat_axis=1, tiled=True),
    )
    per_source = got_count[0] * (HB // group_size)
    ends_at = jnp.cumsum(per_source)
    target_ids = jnp.arange(HB, dtype=jnp.int32)
    before_mask = ends_at[None, :] <= target_ids[:, None]
    source_ids = jnp.sum(before_mask.astype(jnp.int32), axis=1)
    begins_at = jnp.sum(jnp.where(before_mask, per_source[None, :], 0), axis=1)
    pick_ids = (target_ids - begins_at) * group_size + source_ids
    rows_earn = jnp.take(got_earn.reshape(source_rows * group_size, num_periods), pick_ids, axis=0)
    rows_start = jnp.take(got_start.reshape(source_rows * group_size), pick_ids)
    rows_len = jnp.take(got_len.reshape(source_rows * group_size), pick_ids)
    row_live = jnp.ones((HB,), dtype=bool)
    years_local = jnp.sum(jnp.where(row_live, rows_len, 0)).astype(jnp.float32)
    row_total_count = rows_earn.shape[0]
    columns = rows_earn.T
    period_ids = jnp.arange(num_periods, dtype=jnp.int32)

    def observed(step_now):
        return row_live & (step_now >= rows_start) & (step_now < rows_start + rows_len)

    def forward(prev_alpha, inputs):
        matrix, column, step_now = inputs
        fresh_start = (step_now <= rows_start)[:, None]
        moved_mass = jnp.dot(
            prev_alpha, matrix, precision=top_precision, preferred_element_type=jnp.float32
        )
        joint_mass = jnp.where(fresh_start, first_probs[None, :], moved_mass) * emission(
            column, state_mean, log_sd
        )
        seen_now = observed(step_now)
        scale_now = jnp.where(seen_now, jnp.sum(joint_mass, axis=1), 1.0)
        new_alpha = jnp.where(seen_now[:, None], joint_mass / scale_now[:, None], prev_alpha)
        return (new_alpha, (new_alpha, scale_now))

    start_alpha = jnp.broadcast_to(first_probs[None, :], (row_total_count, num_states))
    _, (alphas, scales) = lax.scan(forward, start_alpha, (trans_probs, columns, period_ids))

    def carry_of(back_now, column, scale_now, step_now):
        seen_now = observed(step_now)
        return jnp.where(
            seen_now[:, None],
            emission(column, state_mean, log_sd) * back_now / scale_now[:, None],
            0.0,
        )

    def backward(carry_now, inputs):
        matrix, alpha_prev, column_prev, scale_prev, step_now = inputs
        moving = row_live & (step_now > rows_start) & (step_now < rows_start + rows_len)
        weights = jnp.where(moving[:, None], alpha_prev, 0.0)
        own_carry = lax.dynamic_slice_in_dim(carry_now, lead_state, half_states, 1)
        grad_term = lax.dot_general(
            weights,
            own_carry,
            (((0,), (0,)), ((), ())),
            precision=top_precision,
            preferred_element_type=jnp.float32,
        )
        pulled = lax.dot_general(
            carry_now,
            matrix,
            (((1,), (1,)), ((), ())),
            precision=top_precision,
            preferred_element_type=jnp.float32,
        )
        back_now = jnp.where(moving[:, None], pulled, 1.0)
        return (carry_of(back_now, column_prev, scale_prev, step_now - 1), grad_term)

    ones_back = jnp.ones((row_total_count, num_states), jnp.float32)
    last_carry = carry_of(
        ones_back, columns[num_periods - 1], scales[num_periods - 1], num_periods - 1
    )
    _, grad_terms = lax.scan(
        backward,
        last_carry,
        (trans_probs[1:], alphas[:-1], columns[:-1], scales[:-1], period_ids[1:]),
        reverse=True,
    )
    zero_first = jnp.zeros((1,) + grad_terms.shape[1:], jnp.float32)
    partial_counts = jnp.concatenate([zero_first, grad_terms], axis=0)
    loglik_local = jnp.sum(jnp.log(scales))
    summed = lax.psum_scatter(partial_counts, "hh", scatter_dimension=1, tiled=True)
    summed = lax.psum_scatter(summed, "per", scatter_dimension=0, tiled=True)
    loglik_share = loglik_local / core_count
    years_share = years_local / core_count
    period_block = summed.shape[0]
    row_block_size = summed.shape[1]
    local_probs = lax.dynamic_slice(
        trans_probs,
        (lax.axis_index("per") * period_block, lax.axis_index("hh") * row_block_size, lead_state),
        (period_block, row_block_size, half_states),
    )
    weighted = local_probs * summed
    row_total, loglik_core, years_core = lax.psum(
        (jnp.sum(weighted, axis=2), loglik_share, years_share), "st"
    )
    loglik_all, years_all = lax.psum((loglik_core, years_core), ("hh", "per"))
    factor = float(num_states * num_states * num_periods) / years_all
    trans_grad = factor * (weighted - local_probs * row_total[:, :, None])
    mean_loglik = jnp.reshape(loglik_all / years_all, (1,))
    return (trans_grad, mean_loglik)


F32 = jnp.float32
BF = jnp.bfloat16
MESH = pl.DeviceIdType.MESH


def split_hi_lo(v):
    hi = v.astype(BF)
    return hi, (v - hi.astype(F32)).astype(BF)


def dot3(a, hi, lo, dims):
    ah, al = split_hi_lo(a)
    dd = lambda p, q: lax.dot_general(p, q, (dims, ((), ())), preferred_element_type=F32)
    return dd(ah, hi) + (dd(al, hi) + dd(ah, lo))


def three_way(v):
    hi = v.astype(BF)
    rest = v - hi.astype(F32)
    mid = rest.astype(BF)
    return hi, mid, (rest - mid.astype(F32)).astype(BF)


def sum3(pieces, right, dims):
    dd = lambda p: lax.dot_general(p, right, (dims, ((), ())), preferred_element_type=F32)
    return (dd(pieces[0]) + dd(pieces[1])) + dd(pieces[2])


def fused_kernel(cfg, earn, begin, length, count, logits, init_ref, mean_ref, sd_ref, out, llout,
                 pack, got, people, lg, phi, plo, amem, bmem, xsend, xrecv, cacc, crecv,
                 llbox, rts, rtr,
                 hs_sem, hr_sem, lr_sem, ls_sem, xs_sem, xr_sem, c_sem, r_sem, lls_sem, llr_sem):
    nz, nt, half_t, own_t, rows, num_states, blocks = cfg
    x = lax.axis_index("per")
    z = lax.axis_index("hh")
    s = lax.axis_index("st")
    half = num_states // 2
    nsrc = nz * 2
    zr = num_states // nz
    per_half = half // zr
    slots = earn.shape[1]
    slab = slots // 2
    wide_slab = pack.shape[1]

    def rcopy(src, dst, ss, rs, dev):
        return pltpu.make_async_remote_copy(
            src_ref=src, dst_ref=dst, send_sem=ss, recv_sem=rs,
            device_id=dev, device_id_type=MESH)

    partner = {"hh": z, "per": x, "st": 1 - s}
    across = {"hh": z, "per": 1 - x, "st": s}
    corner = {"hh": z, "per": 1 - x, "st": 1 - s}
    peers = []
    for dz in range(nz):
        for dx in range(2):
            if dz or dx:
                peers.append({"hh": lax.rem(z + dz, nz), "per": lax.rem(x + dx, 2), "st": s})
    barrier = pltpu.get_barrier_semaphore()
    for dev in peers + [partner, corner]:
        pl.semaphore_signal(barrier, inc=1, device_id=dev, device_id_type=MESH)

    local = []
    for i in range(own_t):
        c = pltpu.make_async_copy(logits.at[i], lg.at[own_t * s + i], lr_sem.at[i])
        c.start()
        local.append(c)

    cnt = count[0].astype(F32)
    spot = lax.broadcasted_iota(jnp.int32, (1, slots), 1).astype(F32)
    lens = length[...].astype(F32)
    own_years = jnp.sum(jnp.where(spot < cnt * float(rows), lens, 0.0), axis=1, keepdims=True)
    table = jnp.concatenate(
        [earn[...], begin[...].astype(F32), lens, jnp.full((1, slots), 1.0, F32) * cnt,
         jnp.broadcast_to(own_years, (1, slots)), jnp.zeros((4, slots), F32)], axis=0)
    q_id = lax.broadcasted_iota(jnp.int32, (slots, wide_slab), 0)
    r_id = lax.broadcasted_iota(jnp.int32, (slots, wide_slab), 1)
    pick = jnp.where((q_id == r_id * 2 + s) & (r_id < slab), 1.0, 0.0).astype(BF)
    pack[...] = sum3(three_way(table), pick, ((1,), (0,)))
    pl.semaphore_wait(barrier, len(peers) + 2)

    me_src = z * 2 + x
    hist = [pltpu.make_async_copy(pack, got.at[me_src], hr_sem.at[0])]
    hist[0].start()
    for n, dev in enumerate(peers):
        c = rcopy(pack, got.at[me_src], hs_sem.at[n], hr_sem.at[n + 1], dev)
        c.start()
        hist.append(c)
    near = []
    for i in range(own_t):
        c = rcopy(logits.at[i], lg.at[own_t * s + i], ls_sem.at[i], lr_sem.at[own_t + i], partner)
        c.start()
        near.append(c)

    mean = mean_ref[...]
    log_sd = sd_ref[...]
    raised_first = jnp.exp(init_ref[...])
    first = raised_first / jnp.sum(raised_first, axis=1, keepdims=True)
    inv_sd = jnp.exp(-log_sd)

    def make_probs(l):
        r = jnp.exp(lg[l].astype(F32))
        hi, lo = split_hi_lo(r / jnp.sum(r, axis=1, keepdims=True))
        phi[l] = hi
        plo[l] = lo

    for i in range(own_t):
        local[i].wait()
        make_probs(own_t * s + i)
    cacc[...] = jnp.zeros(cacc.shape, F32)
    for i in range(own_t):
        near[i].wait_recv()
        make_probs(own_t * (1 - s) + i)

    hist[0].wait()
    for n in range(len(peers)):
        hist[n + 1].wait_recv()
    base = jnp.zeros((1, 1), F32)
    years = jnp.zeros((1, 1), F32)
    bases, lives = [], []
    for src in range(nsrc):
        live = got[src, nt + 2:nt + 3, 0:1] * float(rows // 2)
        years = years + got[src, nt + 3:nt + 4, 0:1]
        bases.append(base)
        lives.append(live)
        base = base + live
    g0, g1, g2 = three_way(jnp.concatenate([got[src] for src in range(nsrc)], axis=1))
    seat = lax.broadcasted_iota(jnp.int32, (rows, wide_slab), 0).astype(F32)
    lane = lax.broadcasted_iota(jnp.int32, (rows, wide_slab), 1).astype(F32)
    for b in range(blocks):
        hot = jnp.concatenate(
            [jnp.where((lane + (bases[src] - float(b * rows)) == seat) & (lane < lives[src]), 1.0, 0.0).astype(BF)
             for src in range(nsrc)], axis=1)
        dd = lambda g: lax.dot_general(hot, g, (((1,), (1,)), ((), ())), preferred_element_type=F32)
        people[b, :, 0:nt + 8] = (dd(g0) + dd(g1)) + dd(g2)

    def emit(b, t):
        zs = (people[b, :, t:t + 1] - mean) * inv_sd
        return jnp.exp(-0.5 * zs * zs - log_sd)

    def span(b):
        start = people[b, :, nt:nt + 1]
        return start, start + people[b, :, nt + 1:nt + 2]

    def add_counts(k, a, u):
        part = lax.dot_general(a.astype(BF), u.astype(BF), (((0,), (0,)), ((), ())),
                               preferred_element_type=F32)
        cacc[k, 0] += part[:, :half]
        cacc[k, 1] += part[:, half:]

    def send_across(b, v):
        xsend[b] = v.astype(BF)
        rcopy(xsend.at[b], xrecv.at[b], xs_sem.at[b], xr_sem.at[b], across).start()

    def take_across(b):
        c = rcopy(xsend.at[b], xrecv.at[b], xs_sem.at[b], xr_sem.at[b], across)
        c.wait_recv()
        return xrecv[b].astype(F32)

    def chosen(v):
        return jnp.where(z // per_half == 0, v[:, :half], v[:, half:])

    def forward_step(b, t, prev, prev_inv, total, start, stop):
        e = emit(b, t)
        moved = None
        if t == 0:
            joint = first * e
        else:
            l = t % half_t
            moved = dot3(prev, phi[l], plo[l], ((1,), (0,))) * prev_inv
            joint = jnp.where(float(t) <= start, first, moved) * e
        scale = jnp.sum(joint, axis=1, keepdims=True)
        seen = (float(t) >= start) & (float(t) < stop)
        total = total + jnp.where(seen, jnp.log(scale), 0.0)
        return joint, 1.0 / scale, total, moved

    def backward_step(b, t, back, start, stop, last):
        v = emit(b, t) * back
        norm_inv = 1.0 / jnp.sum(v, axis=1, keepdims=True)
        mv = (float(t) > start) & (float(t) < stop)
        u = jnp.where(mv, v * norm_inv, 0.0)
        if not last:
            l = t % half_t
            back = jnp.where(mv, dot3(v, phi[l], plo[l], ((1,), (1,))) * norm_inv, 1.0)
        return u, back, mv

    def weight(mv, zsum):
        return jnp.where(mv, 1.0 / jnp.where(mv, zsum, 1.0), 0.0)

    def put_ll(total):
        llbox[x * 2 + s] = jnp.broadcast_to(jnp.sum(total, axis=0, keepdims=True), (8, 128))

    @pl.when(x == 0)
    def _early():
        def one(b, total):
            start, stop = span(b)
            prev = prev_inv = None
            for t in range(half_t):
                prev, prev_inv, total, moved = forward_step(b, t, prev, prev_inv, total, start, stop)
                if t > 0:
                    bmem[b, t] = moved
                if t < half_t - 1:
                    amem[b, t + 1, :, 0:half] = chosen(prev) * prev_inv
            send_across(b, prev * prev_inv)
            return total

        put_ll(lax.fori_loop(0, blocks, one, jnp.zeros((rows, 1), F32)))

        def two(b, carry):
            start, stop = span(b)
            back = take_across(b)
            for t in range(half_t - 1, 0, -1):
                u, back, mv = backward_step(b, t, back, start, stop, t == 1)
                w = weight(mv, jnp.sum(bmem[b, t] * u, axis=1, keepdims=True))
                add_counts(t, amem[b, t, :, 0:half] * w, u)
            return carry

        lax.fori_loop(0, blocks, two, 0)

    @pl.when(x == 1)
    def _late():
        def one(b, carry):
            start, stop = span(b)
            back = jnp.ones((rows, num_states), F32)
            for t in range(nt - 1, half_t - 1, -1):
                u, back, mv = backward_step(b, t, back, start, stop, False)
                amem[b, t - half_t] = u
                bmem[b, t - half_t] = back
            send_across(b, back)
            return carry

        lax.fori_loop(0, blocks, one, 0)

        def two(b, total):
            start, stop = span(b)
            prev = take_across(b)
            prev_inv = jnp.ones((rows, 1), F32)
            for t in range(half_t, nt):
                alpha = prev * prev_inv
                mv = (float(t) > start) & (float(t) < stop)
                w = weight(mv, jnp.sum(bmem[b, t - half_t] * alpha, axis=1, keepdims=True))
                add_counts(t - half_t, chosen(alpha) * w, amem[b, t - half_t])
                prev, prev_inv, total, moved = forward_step(b, t, prev, prev_inv, total, start, stop)
            return total

        put_ll(lax.fori_loop(0, blocks, two, jnp.zeros((rows, 1), F32)))

    mine = x * 2 + s
    ll_to = [(partner, x * 2 + 1 - s), (across, (1 - x) * 2 + s), (corner, (1 - x) * 2 + 1 - s)]
    ll_copies = []
    for j, (dev, there) in enumerate(ll_to):
        c = rcopy(llbox.at[mine], llbox.at[mine], lls_sem.at[j], llr_sem.at[j], dev)
        c.start()
        ll_copies.append(c)
    zrow = pl.ds(pl.multiple_of(lax.rem(z, per_half) * zr, 8), zr)
    prow = pl.ds(pl.multiple_of(z * zr, 8), zr)
    cc = rcopy(cacc.at[:, 1 - s, zrow], crecv, c_sem.at[0], c_sem.at[1], partner)
    cc.start()
    lane_out = lax.broadcasted_iota(jnp.int32, (zr, 128), 1)
    sums = jnp.zeros((zr, 128), F32)
    for k in range(half_t):
        r = jnp.exp(lg[k, prow, :].astype(F32))
        pr = r / jnp.sum(r, axis=1, keepdims=True)
        row = jnp.sum(pr[:, :half] * cacc[k, 0, zrow, :] + pr[:, half:] * cacc[k, 1, zrow, :],
                      axis=1, keepdims=True)
        sums = sums + jnp.where(lane_out == k, row, 0.0)
        out[k] = jnp.where(s == 0, pr[:, :half], pr[:, half:])
    rts[...] = sums
    rc = rcopy(rts, rtr, r_sem.at[0], r_sem.at[1], partner)
    rc.start()
    factor = float(num_states * num_states * nt) / years
    cc.wait_recv()
    rc.wait_recv()
    rtot = rts[...] + rtr[...]
    for k in range(half_t):
        out[k] = factor * (out[k] * ((cacc[k, s, zrow, :] + crecv[k]) - rtot[:, k:k + 1]))
    for c in ll_copies:
        c.wait_recv()
    ll = (llbox[0, 0:1, :] + llbox[1, 0:1, :]) + (llbox[2, 0:1, :] + llbox[3, 0:1, :])
    llout[...] = ll / years

    for c in hist[1:] + near + ll_copies + [cc, rc]:
        c.wait_send()
    for b in range(blocks):
        rcopy(xsend.at[b], xrecv.at[b], xs_sem.at[b], xr_sem.at[b], across).wait_send()


def fused_device(
    earnings, starts, lengths, block_count, trans_logits, init_logits, state_mean, log_sd
):
    num_states = init_logits.shape[0]
    nt = earnings.shape[1]
    slot_rows = earnings.shape[0]
    nz = lax.axis_size("hh")
    nsrc = nz * 2
    own_t = trans_logits.shape[0]
    half_t = nt // 2
    half = num_states // 2
    zr = num_states // nz
    rows = HB
    blocks = nsrc // 2
    wide_slab = -(-(slot_rows // 2) // 128) * 128
    cfg = (nz, nt, half_t, own_t, rows, num_states, blocks)
    V = pltpu.VMEM
    D = pltpu.SemaphoreType.DMA
    vm = pl.BlockSpec(memory_space=pltpu.VMEM)
    grad, ll = pl.pallas_call(
        functools.partial(fused_kernel, cfg),
        out_shape=(jax.ShapeDtypeStruct((half_t, zr, half), F32),
                   jax.ShapeDtypeStruct((1, 128), F32)),
        in_specs=[vm, vm, vm, pl.BlockSpec(memory_space=pltpu.SMEM), pl.BlockSpec(memory_space=pl.ANY), vm, vm, vm],
        out_specs=(vm, vm),
        scratch_shapes=[
            V((nt + 8, wide_slab), F32),
            V((nsrc, nt + 8, wide_slab), F32),
            V((blocks, rows, 128), F32),
            V((half_t, num_states, num_states), BF),
            V((half_t, num_states, num_states), BF),
            V((half_t, num_states, num_states), BF),
            V((blocks, half_t, rows, num_states), F32),
            V((blocks, half_t, rows, num_states), F32),
            V((blocks, rows, num_states), BF),
            V((blocks, rows, num_states), BF),
            V((half_t, 2, half, half), F32),
            V((half_t, zr, half), F32),
            V((4, 8, 128), F32),
            V((zr, 128), F32),
            V((zr, 128), F32),
            D((nsrc,)), D((nsrc,)), D((2 * own_t,)), D((own_t,)),
            D((blocks,)), D((blocks,)), D((2,)), D((2,)), D((3,)), D((3,)),
        ],
        compiler_params=pltpu.CompilerParams(
            collective_id=0, has_side_effects=True, vmem_limit_bytes=56 * 1024 * 1024),
        name="chain",
    )(earnings.T, starts[None], lengths[None], block_count, trans_logits,
      init_logits[None], state_mean[None], log_sd[None])
    return grad, ll[0, 0:1]


def solution(mesh):
    fits = mesh.shape["per"] == 2 and mesh.shape["st"] == 2 and mesh.shape["hh"] == 4
    body = fused_device if fits else per_device
    placed = (
        P(("hh", "per"), None),
        P(("hh", "per")),
        P(("hh", "per")),
        P(("hh", "per")),
        P(("grp", "per", "st"), None, None),
        P("grp"),
        P("grp"),
        P("grp"),
    )
    return jax.shard_map(
        body,
        mesh=mesh,
        in_specs=placed,
        out_specs=(P(("grp", "per"), "hh", "st"), P("grp")),
        check_vma=False,
    )
```

```python
import functools

import jax
import jax.numpy as jnp
from jax import lax
from jax.sharding import PartitionSpec as P
from jax.experimental import pallas as pl
from jax.experimental.pallas import tpu as pltpu

HB = 128


top_precision = lax.Precision.HIGHEST


def emission(column, state_mean, log_sd):
    z_score = (column[:, None] - state_mean[None, :]) / jnp.exp(log_sd)[None, :]
    return jnp.exp(-0.5 * z_score * z_score - log_sd[None, :])


def per_device(
    earnings, starts, lengths, block_count, trans_logits, init_logits, state_mean, log_sd
):
    num_states = init_logits.shape[0]
    num_periods = earnings.shape[1]
    slot_rows = earnings.shape[0]
    group_size = lax.axis_size(("hh", "per"))
    core_count = lax.axis_size("st")
    half_states = num_states // core_count
    lead_state = lax.axis_index("st") * half_states
    whole_logits = lax.all_gather(trans_logits, ("per", "st"), axis=0, tiled=True)
    raised = jnp.exp(whole_logits.astype(jnp.float32))
    trans_probs = raised / jnp.sum(raised, axis=2, keepdims=True)
    raised_first = jnp.exp(init_logits)
    first_probs = raised_first / jnp.sum(raised_first)
    source_rows = slot_rows // group_size
    count_out = jnp.broadcast_to(block_count.reshape(1, 1), (1, group_size))
    got_earn, got_start, got_len, got_count = (
        lax.all_to_all(
            earnings.reshape(source_rows, group_size, num_periods),
            ("hh", "per"),
            split_axis=1,
            concat_axis=1,
            tiled=True,
        ),
        lax.all_to_all(
            starts.reshape(source_rows, group_size),
            ("hh", "per"),
            split_axis=1,
            concat_axis=1,
            tiled=True,
        ),
        lax.all_to_all(
            lengths.reshape(source_rows, group_size),
            ("hh", "per"),
            split_axis=1,
            concat_axis=1,
            tiled=True,
        ),
        lax.all_to_all(count_out, ("hh", "per"), split_axis=1, concat_axis=1, tiled=True),
    )
    per_source = got_count[0] * (HB // group_size)
    ends_at = jnp.cumsum(per_source)
    target_ids = jnp.arange(HB, dtype=jnp.int32)
    before_mask = ends_at[None, :] <= target_ids[:, None]
    source_ids = jnp.sum(before_mask.astype(jnp.int32), axis=1)
    begins_at = jnp.sum(jnp.where(before_mask, per_source[None, :], 0), axis=1)
    pick_ids = (target_ids - begins_at) * group_size + source_ids
    rows_earn = jnp.take(got_earn.reshape(source_rows * group_size, num_periods), pick_ids, axis=0)
    rows_start = jnp.take(got_start.reshape(source_rows * group_size), pick_ids)
    rows_len = jnp.take(got_len.reshape(source_rows * group_size), pick_ids)
    row_live = jnp.ones((HB,), dtype=bool)
    years_local = jnp.sum(jnp.where(row_live, rows_len, 0)).astype(jnp.float32)
    row_total_count = rows_earn.shape[0]
    columns = rows_earn.T
    period_ids = jnp.arange(num_periods, dtype=jnp.int32)

    def observed(step_now):
        return row_live & (step_now >= rows_start) & (step_now < rows_start + rows_len)

    def forward(prev_alpha, inputs):
        matrix, column, step_now = inputs
        fresh_start = (step_now <= rows_start)[:, None]
        moved_mass = jnp.dot(
            prev_alpha, matrix, precision=top_precision, preferred_element_type=jnp.float32
        )
        joint_mass = jnp.where(fresh_start, first_probs[None, :], moved_mass) * emission(
            column, state_mean, log_sd
        )
        seen_now = observed(step_now)
        scale_now = jnp.where(seen_now, jnp.sum(joint_mass, axis=1), 1.0)
        new_alpha = jnp.where(seen_now[:, None], joint_mass / scale_now[:, None], prev_alpha)
        return (new_alpha, (new_alpha, scale_now))

    start_alpha = jnp.broadcast_to(first_probs[None, :], (row_total_count, num_states))
    _, (alphas, scales) = lax.scan(forward, start_alpha, (trans_probs, columns, period_ids))

    def carry_of(back_now, column, scale_now, step_now):
        seen_now = observed(step_now)
        return jnp.where(
            seen_now[:, None],
            emission(column, state_mean, log_sd) * back_now / scale_now[:, None],
            0.0,
        )

    def backward(carry_now, inputs):
        matrix, alpha_prev, column_prev, scale_prev, step_now = inputs
        moving = row_live & (step_now > rows_start) & (step_now < rows_start + rows_len)
        weights = jnp.where(moving[:, None], alpha_prev, 0.0)
        own_carry = lax.dynamic_slice_in_dim(carry_now, lead_state, half_states, 1)
        grad_term = lax.dot_general(
            weights,
            own_carry,
            (((0,), (0,)), ((), ())),
            precision=top_precision,
            preferred_element_type=jnp.float32,
        )
        pulled = lax.dot_general(
            carry_now,
            matrix,
            (((1,), (1,)), ((), ())),
            precision=top_precision,
            preferred_element_type=jnp.float32,
        )
        back_now = jnp.where(moving[:, None], pulled, 1.0)
        return (carry_of(back_now, column_prev, scale_prev, step_now - 1), grad_term)

    ones_back = jnp.ones((row_total_count, num_states), jnp.float32)
    last_carry = carry_of(
        ones_back, columns[num_periods - 1], scales[num_periods - 1], num_periods - 1
    )
    _, grad_terms = lax.scan(
        backward,
        last_carry,
        (trans_probs[1:], alphas[:-1], columns[:-1], scales[:-1], period_ids[1:]),
        reverse=True,
    )
    zero_first = jnp.zeros((1,) + grad_terms.shape[1:], jnp.float32)
    partial_counts = jnp.concatenate([zero_first, grad_terms], axis=0)
    loglik_local = jnp.sum(jnp.log(scales))
    summed = lax.psum_scatter(partial_counts, "hh", scatter_dimension=1, tiled=True)
    summed = lax.psum_scatter(summed, "per", scatter_dimension=0, tiled=True)
    loglik_share = loglik_local / core_count
    years_share = years_local / core_count
    period_block = summed.shape[0]
    row_block_size = summed.shape[1]
    local_probs = lax.dynamic_slice(
        trans_probs,
        (lax.axis_index("per") * period_block, lax.axis_index("hh") * row_block_size, lead_state),
        (period_block, row_block_size, half_states),
    )
    weighted = local_probs * summed
    row_total, loglik_core, years_core = lax.psum(
        (jnp.sum(weighted, axis=2), loglik_share, years_share), "st"
    )
    loglik_all, years_all = lax.psum((loglik_core, years_core), ("hh", "per"))
    factor = float(num_states * num_states * num_periods) / years_all
    trans_grad = factor * (weighted - local_probs * row_total[:, :, None])
    mean_loglik = jnp.reshape(loglik_all / years_all, (1,))
    return (trans_grad, mean_loglik)


F32 = jnp.float32
BF = jnp.bfloat16
MESH = pl.DeviceIdType.MESH


def split_hi_lo(v):
    hi = v.astype(BF)
    return hi, (v - hi.astype(F32)).astype(BF)


def dot3(a, hi, lo, dims):
    ah, al = split_hi_lo(a)
    dd = lambda p, q: lax.dot_general(p, q, (dims, ((), ())), preferred_element_type=F32)
    return dd(ah, hi) + (dd(al, hi) + dd(ah, lo))


def three_way(v):
    hi = v.astype(BF)
    rest = v - hi.astype(F32)
    mid = rest.astype(BF)
    return hi, mid, (rest - mid.astype(F32)).astype(BF)


def sum3(pieces, right, dims):
    dd = lambda p: lax.dot_general(p, right, (dims, ((), ())), preferred_element_type=F32)
    return (dd(pieces[0]) + dd(pieces[1])) + dd(pieces[2])


def fused_kernel(cfg, earn, begin, length, count, logits, init_ref, mean_ref, sd_ref, out, llout,
                 pack, got, people, lg, phi, plo, amem, bmem, xsend, xrecv, cacc, crecv,
                 llbox, rts, rtr,
                 hs_sem, hr_sem, lr_sem, ls_sem, xs_sem, xr_sem, c_sem, r_sem, lls_sem, llr_sem):
    nz, nt, half_t, own_t, held, rows, num_states, blocks = cfg
    x = lax.axis_index("per")
    z = lax.axis_index("hh")
    s = lax.axis_index("st")
    half = num_states // 2
    nsrc = nz * 2
    zr = num_states // nz
    per_half = half // zr
    slots = earn.shape[1]
    slab = slots // 2
    wide_slab = pack.shape[1]

    def rcopy(src, dst, ss, rs, dev):
        return pltpu.make_async_remote_copy(
            src_ref=src, dst_ref=dst, send_sem=ss, recv_sem=rs,
            device_id=dev, device_id_type=MESH)

    partner = {"hh": z, "per": x, "st": 1 - s}
    across = {"hh": z, "per": 1 - x, "st": s}
    corner = {"hh": z, "per": 1 - x, "st": 1 - s}
    peers = []
    for dz in range(nz):
        for dx in range(2):
            if dz or dx:
                peers.append({"hh": lax.rem(z + dz, nz), "per": lax.rem(x + dx, 2), "st": s})
    barrier = pltpu.get_barrier_semaphore()
    for dev in peers + [partner, corner]:
        pl.semaphore_signal(barrier, inc=1, device_id=dev, device_id_type=MESH)

    local = []
    for i in range(own_t):
        c = pltpu.make_async_copy(logits.at[i], lg.at[own_t * s + i], lr_sem.at[i])
        c.start()
        local.append(c)

    cnt = count[0].astype(F32)
    spot = lax.broadcasted_iota(jnp.int32, (1, slots), 1).astype(F32)
    lens = length[...].astype(F32)
    own_years = jnp.sum(jnp.where(spot < cnt * float(held), lens, 0.0), axis=1, keepdims=True)
    table = jnp.concatenate(
        [earn[...], begin[...].astype(F32), lens, jnp.full((1, slots), 1.0, F32) * cnt,
         jnp.broadcast_to(own_years, (1, slots)), jnp.zeros((4, slots), F32)], axis=0)
    q_id = lax.broadcasted_iota(jnp.int32, (slots, wide_slab), 0)
    r_id = lax.broadcasted_iota(jnp.int32, (slots, wide_slab), 1)
    pick = jnp.where((q_id == r_id * 2 + s) & (r_id < slab), 1.0, 0.0).astype(BF)
    pack[...] = sum3(three_way(table), pick, ((1,), (0,)))
    pl.semaphore_wait(barrier, len(peers) + 2)

    me_src = z * 2 + x
    hist = [pltpu.make_async_copy(pack, got.at[me_src], hr_sem.at[0])]
    hist[0].start()
    for n, dev in enumerate(peers):
        c = rcopy(pack, got.at[me_src], hs_sem.at[n], hr_sem.at[n + 1], dev)
        c.start()
        hist.append(c)
    near = []
    for i in range(own_t):
        c = rcopy(logits.at[i], lg.at[own_t * s + i], ls_sem.at[i], lr_sem.at[own_t + i], partner)
        c.start()
        near.append(c)

    mean = mean_ref[...]
    log_sd = sd_ref[...]
    raised_first = jnp.exp(init_ref[...])
    first = raised_first / jnp.sum(raised_first, axis=1, keepdims=True)
    inv_sd = jnp.exp(-log_sd)

    def make_probs(l):
        r = jnp.exp(lg[l].astype(F32))
        hi, lo = split_hi_lo(r / jnp.sum(r, axis=1, keepdims=True))
        phi[l] = hi
        plo[l] = lo

    for i in range(own_t):
        local[i].wait()
        make_probs(own_t * s + i)
    cacc[...] = jnp.zeros(cacc.shape, F32)
    for i in range(own_t):
        near[i].wait_recv()
        make_probs(own_t * (1 - s) + i)

    hist[0].wait()
    for n in range(len(peers)):
        hist[n + 1].wait_recv()
    base = jnp.zeros((1, 1), F32)
    years = jnp.zeros((1, 1), F32)
    bases, lives = [], []
    for src in range(nsrc):
        live = got[src, nt + 2:nt + 3, 0:1] * float(held // 2)
        years = years + got[src, nt + 3:nt + 4, 0:1]
        bases.append(base)
        lives.append(live)
        base = base + live
    g0, g1, g2 = three_way(jnp.concatenate([got[src] for src in range(nsrc)], axis=1))
    seat = lax.broadcasted_iota(jnp.int32, (rows, wide_slab), 0).astype(F32)
    lane = lax.broadcasted_iota(jnp.int32, (rows, wide_slab), 1).astype(F32)
    for b in range(blocks):
        hot = jnp.concatenate(
            [jnp.where((lane + (bases[src] - float(b * rows)) == seat) & (lane < lives[src]), 1.0, 0.0).astype(BF)
             for src in range(nsrc)], axis=1)
        dd = lambda g: lax.dot_general(hot, g, (((1,), (1,)), ((), ())), preferred_element_type=F32)
        people[b, :, 0:nt + 8] = (dd(g0) + dd(g1)) + dd(g2)

    def emit(b, t):
        zs = (people[b, :, t:t + 1] - mean) * inv_sd
        return jnp.exp(-0.5 * zs * zs - log_sd)

    def span(b):
        start = people[b, :, nt:nt + 1]
        return start, start + people[b, :, nt + 1:nt + 2]

    def add_counts(k, a, u):
        part = lax.dot_general(a.astype(BF), u.astype(BF), (((0,), (0,)), ((), ())),
                               preferred_element_type=F32)
        cacc[k, 0] += part[:, :half]
        cacc[k, 1] += part[:, half:]

    def send_across(b, v):
        xsend[b] = v
        rcopy(xsend.at[b], xrecv.at[b], xs_sem.at[b], xr_sem.at[b], across).start()

    def take_across(b):
        c = rcopy(xsend.at[b], xrecv.at[b], xs_sem.at[b], xr_sem.at[b], across)
        c.wait_recv()
        return xrecv[b]

    def chosen(v):
        return jnp.where(z // per_half == 0, v[:, :half], v[:, half:])

    def forward_step(b, t, prev, prev_inv, total, start, stop):
        e = emit(b, t)
        moved = None
        if t == 0:
            joint = first * e
        else:
            l = t % half_t
            moved = dot3(prev, phi[l], plo[l], ((1,), (0,))) * prev_inv
            joint = jnp.where(float(t) <= start, first, moved) * e
        scale = jnp.sum(joint, axis=1, keepdims=True)
        seen = (float(t) >= start) & (float(t) < stop)
        total = total + jnp.where(seen, jnp.log(scale), 0.0)
        return joint, 1.0 / scale, total, moved

    def backward_step(b, t, back, start, stop, last):
        v = emit(b, t) * back
        norm_inv = 1.0 / jnp.sum(v, axis=1, keepdims=True)
        mv = (float(t) > start) & (float(t) < stop)
        u = jnp.where(mv, v * norm_inv, 0.0)
        if not last:
            l = t % half_t
            back = jnp.where(mv, dot3(v, phi[l], plo[l], ((1,), (1,))) * norm_inv, 1.0)
        return u, back, mv

    def weight(mv, zsum):
        return jnp.where(mv, 1.0 / jnp.where(mv, zsum, 1.0), 0.0)

    def put_ll(total):
        llbox[x * 2 + s] = jnp.broadcast_to(jnp.sum(total, axis=0, keepdims=True), (8, 128))

    @pl.when(x == 0)
    def _early():
        def one(b, total):
            start, stop = span(b)
            prev = prev_inv = None
            for t in range(half_t):
                prev, prev_inv, total, moved = forward_step(b, t, prev, prev_inv, total, start, stop)
                if t > 0:
                    bmem[b, t] = moved
                if t < half_t - 1:
                    amem[b, t + 1, :, 0:half] = chosen(prev) * prev_inv
            send_across(b, prev * prev_inv)
            return total

        put_ll(lax.fori_loop(0, blocks, one, jnp.zeros((rows, 1), F32)))

        def two(b, carry):
            start, stop = span(b)
            back = take_across(b)
            for t in range(half_t - 1, 0, -1):
                u, back, mv = backward_step(b, t, back, start, stop, t == 1)
                w = weight(mv, jnp.sum(bmem[b, t] * u, axis=1, keepdims=True))
                add_counts(t, amem[b, t, :, 0:half] * w, u)
            return carry

        lax.fori_loop(0, blocks, two, 0)

    @pl.when(x == 1)
    def _late():
        def one(b, carry):
            start, stop = span(b)
            back = jnp.ones((rows, num_states), F32)
            for t in range(nt - 1, half_t - 1, -1):
                u, back, mv = backward_step(b, t, back, start, stop, False)
                amem[b, t - half_t] = u
                bmem[b, t - half_t] = back
            send_across(b, back)
            return carry

        lax.fori_loop(0, blocks, one, 0)

        def two(b, total):
            start, stop = span(b)
            prev = take_across(b)
            prev_inv = jnp.ones((rows, 1), F32)
            for t in range(half_t, nt):
                alpha = prev * prev_inv
                mv = (float(t) > start) & (float(t) < stop)
                w = weight(mv, jnp.sum(bmem[b, t - half_t] * alpha, axis=1, keepdims=True))
                add_counts(t - half_t, chosen(alpha) * w, amem[b, t - half_t])
                prev, prev_inv, total, moved = forward_step(b, t, prev, prev_inv, total, start, stop)
            return total

        put_ll(lax.fori_loop(0, blocks, two, jnp.zeros((rows, 1), F32)))

    mine = x * 2 + s
    ll_to = [(partner, x * 2 + 1 - s), (across, (1 - x) * 2 + s), (corner, (1 - x) * 2 + 1 - s)]
    ll_copies = []
    for j, (dev, there) in enumerate(ll_to):
        c = rcopy(llbox.at[mine], llbox.at[mine], lls_sem.at[j], llr_sem.at[j], dev)
        c.start()
        ll_copies.append(c)
    zrow = pl.ds(pl.multiple_of(lax.rem(z, per_half) * zr, 8), zr)
    prow = pl.ds(pl.multiple_of(z * zr, 8), zr)
    cc = rcopy(cacc.at[:, 1 - s, zrow], crecv, c_sem.at[0], c_sem.at[1], partner)
    cc.start()
    lane_out = lax.broadcasted_iota(jnp.int32, (zr, 128), 1)
    sums = jnp.zeros((zr, 128), F32)
    for k in range(half_t):
        r = jnp.exp(lg[k, prow, :].astype(F32))
        pr = r / jnp.sum(r, axis=1, keepdims=True)
        row = jnp.sum(pr[:, :half] * cacc[k, 0, zrow, :] + pr[:, half:] * cacc[k, 1, zrow, :],
                      axis=1, keepdims=True)
        sums = sums + jnp.where(lane_out == k, row, 0.0)
        out[k] = jnp.where(s == 0, pr[:, :half], pr[:, half:])
    rts[...] = sums
    rc = rcopy(rts, rtr, r_sem.at[0], r_sem.at[1], partner)
    rc.start()
    factor = float(num_states * num_states * nt) / years
    cc.wait_recv()
    rc.wait_recv()
    rtot = rts[...] + rtr[...]
    for k in range(half_t):
        out[k] = factor * (out[k] * ((cacc[k, s, zrow, :] + crecv[k]) - rtot[:, k:k + 1]))
    for c in ll_copies:
        c.wait_recv()
    ll = (llbox[0, 0:1, :] + llbox[1, 0:1, :]) + (llbox[2, 0:1, :] + llbox[3, 0:1, :])
    llout[...] = ll / years

    for c in hist[1:] + near + ll_copies + [cc, rc]:
        c.wait_send()
    for b in range(blocks):
        rcopy(xsend.at[b], xrecv.at[b], xs_sem.at[b], xr_sem.at[b], across).wait_send()


def fused_device(
    earnings, starts, lengths, block_count, trans_logits, init_logits, state_mean, log_sd
):
    num_states = init_logits.shape[0]
    nt = earnings.shape[1]
    slot_rows = earnings.shape[0]
    nz = lax.axis_size("hh")
    nsrc = nz * 2
    own_t = trans_logits.shape[0]
    half_t = nt // 2
    half = num_states // 2
    zr = num_states // nz
    rows = HB * 2
    blocks = nsrc // 4
    wide_slab = -(-(slot_rows // 2) // 128) * 128
    cfg = (nz, nt, half_t, own_t, HB, rows, num_states, blocks)
    V = pltpu.VMEM
    D = pltpu.SemaphoreType.DMA
    vm = pl.BlockSpec(memory_space=pltpu.VMEM)
    grad, ll = pl.pallas_call(
        functools.partial(fused_kernel, cfg),
        out_shape=(jax.ShapeDtypeStruct((half_t, zr, half), F32),
                   jax.ShapeDtypeStruct((1, 128), F32)),
        in_specs=[vm, vm, vm, pl.BlockSpec(memory_space=pltpu.SMEM), pl.BlockSpec(memory_space=pl.ANY), vm, vm, vm],
        out_specs=(vm, vm),
        scratch_shapes=[
            V((nt + 8, wide_slab), F32),
            V((nsrc, nt + 8, wide_slab), F32),
            V((blocks, rows, 128), F32),
            V((half_t, num_states, num_states), BF),
            V((half_t, num_states, num_states), BF),
            V((half_t, num_states, num_states), BF),
            V((blocks, half_t, rows, num_states), F32),
            V((blocks, half_t, rows, num_states), F32),
            V((blocks, rows, num_states), F32),
            V((blocks, rows, num_states), F32),
            V((half_t, 2, half, half), F32),
            V((half_t, zr, half), F32),
            V((4, 8, 128), F32),
            V((zr, 128), F32),
            V((zr, 128), F32),
            D((nsrc,)), D((nsrc,)), D((2 * own_t,)), D((own_t,)),
            D((blocks,)), D((blocks,)), D((2,)), D((2,)), D((3,)), D((3,)),
        ],
        compiler_params=pltpu.CompilerParams(
            collective_id=0, has_side_effects=True, vmem_limit_bytes=56 * 1024 * 1024),
        name="chain",
    )(earnings.T, starts[None], lengths[None], block_count, trans_logits,
      init_logits[None], state_mean[None], log_sd[None])
    return grad, ll[0, 0:1]


def solution(mesh):
    fits = mesh.shape["per"] == 2 and mesh.shape["st"] == 2 and mesh.shape["hh"] == 4
    body = fused_device if fits else per_device
    placed = (
        P(("hh", "per"), None),
        P(("hh", "per")),
        P(("hh", "per")),
        P(("hh", "per")),
        P(("grp", "per", "st"), None, None),
        P("grp"),
        P("grp"),
        P("grp"),
    )
    return jax.shard_map(
        body,
        mesh=mesh,
        in_specs=placed,
        out_specs=(P(("grp", "per"), "hh", "st"), P("grp")),
        check_vma=False,
    )
```
